512 devices in a mesh: narrow: 16 (over x, y_hi, core), wide: 32 (over y_lo, z).
Axes of the slice: x: 4, y: 8 (y_hi: 2, y_lo: 4; y = y_hi * 4 + y_lo), z: 8, core: 2. Of those that a mesh axis runs over, the one named last changes fastest.
Arguments:
- inputs: bfloat16 [128, 2304], P('wide', 'narrow'), may hold values from -6 to 6
- decoder_bias: float32 [2304], replicated, may hold values from -3 to 3
- preactivations: bfloat16 [128, 131072], P(None, ('narrow', 'wide')), may hold values from -6 to 6
- decoder_weight: bfloat16 [131072, 2304], P(('narrow', 'wide')), may hold values from -0.0625 to 0.0625
Outputs:
- grad_encoder: bfloat16 [2304, 131072], P(None, ('narrow', 'wide'))
- grad_decoder: bfloat16 [131072, 2304], P(('narrow', 'wide'))
The draws below stay inside these ranges and needn't reach their ends.
All inputs are finite; a program needn't handle non-finite values.
Results may differ from the reference program's by a relative error of at most 0.0053.
Values may be sent and summed in bfloat16 or wider, within the bound.
No kernel may reach another device: no remote copies, remote signals or barrier semaphores. Data moves between devices by JAX's collectives and lax.ppermute only.
A program may use at most 64 MiB of HBM per device.

```python
import jax
import jax.numpy as jnp

D = 2304
FEATURES = 131072
ROWS = 128


def raised(result, stream_key, source, target, parts, factor):
    def block_of(position):
        return (jnp.arange(result.shape[position]) // (result.shape[position] // parts)).reshape((-1,) + (1,) * (result.ndim - 1 - position))

    one_side = jax.random.permutation(stream_key, parts)[block_of(target)]
    second = (block_of(target) + parts // 2) % parts
    return jnp.where((block_of(source) == one_side) | (block_of(source) == second), factor * result, result)


def block_scale(key, extent, cuts, low, largest):
    def one(dim, parts):
        steps = jax.random.uniform(jax.random.fold_in(jax.random.fold_in(key, 6), dim), (parts,), jnp.float32, low / len(cuts), largest / len(cuts))
        return jnp.repeat(jnp.exp(steps), extent[dim] // parts).reshape((-1,) + (1,) * (len(extent) - dim - 1))

    gain = one(*cuts[0])
    for cut in cuts[1:]:
        gain = gain * one(*cut)
    return gain


def bell_draw(stream_key, dims, spread, limit, pieces=(), kind=jnp.bfloat16):
    values = spread * jax.random.normal(stream_key, dims, jnp.float32)
    if pieces:
        values = values * block_scale(stream_key, dims, pieces, -0.22, 0.18)
    return jnp.clip(values, -limit, limit).astype(kind)


def gaussian_with(stream_key, extent, width, most, cuts, heavy, kind=jnp.bfloat16):
    drawn = width * jax.random.normal(stream_key, extent, jnp.float32)
    if cuts:
        drawn = drawn * block_scale(stream_key, extent, cuts, -0.22, 0.18)
    return jnp.clip(raised(drawn, jax.random.fold_in(stream_key, 3), *heavy), -most, most).astype(kind)


def setup_inputs(seed: int = 0) -> dict:
    keys = jax.random.split(jax.random.key(seed), 5)
    inputs = bell_draw(keys[0], (ROWS, D), 1.0, 6.0, ((0, 32), (1, 16)))
    decoder_bias = bell_draw(keys[1], (D,), 0.5, 3.0, (), jnp.float32)
    preactivations = bell_draw(keys[2], (ROWS, FEATURES), 1.0, 6.0, ((1, 512),))
    decoder_weight = gaussian_with(keys[3], (FEATURES, D), FEATURES ** -0.5, 0.0625, ((0, 512),), (0, 1, 256, 6.0))
    return dict(inputs=inputs, decoder_bias=decoder_bias, preactivations=preactivations, decoder_weight=decoder_weight)


def reference(inputs, decoder_bias, preactivations, decoder_weight):
    hidden = jnp.maximum(preactivations, jnp.zeros_like(preactivations))
    recon = jnp.dot(hidden, decoder_weight, preferred_element_type=jnp.float32) + decoder_bias
    residual = (recon - inputs.astype(jnp.float32)).astype(jnp.bfloat16)
    centered = (inputs.astype(jnp.float32) - decoder_bias).astype(jnp.bfloat16)
    grad_decoder = jnp.dot(hidden.T, residual, preferred_element_type=jnp.float32).astype(jnp.bfloat16)
    backward = jnp.dot(residual, decoder_weight.T, preferred_element_type=jnp.float32)
    masked = jnp.where(preactivations > 0, backward, jnp.zeros_like(backward)).astype(jnp.bfloat16)
    grad_encoder = jnp.dot(centered.T, masked, preferred_element_type=jnp.float32).astype(jnp.bfloat16)
    return grad_encoder, grad_decoder
```

```python
import jax
import jax.numpy as jnp
from jax import lax
from jax.sharding import Mesh, PartitionSpec as P


def swap(x, axis):
    return lax.all_to_all(x, axis, split_axis=0, concat_axis=0, tiled=True)


def to_all(x, axis):
    return swap(jnp.broadcast_to(x[None], (lax.axis_size(axis), *x.shape)), axis)


def shards(inputs, decoder_bias, preactivations, decoder_weight):
    rows, columns = inputs.shape
    narrow = ("pair", "core")
    wide, pairs, cores = (lax.axis_size(a) for a in ("wide", "pair", "core"))
    width = decoder_weight.shape[1]
    half = width // cores
    core = lax.axis_index("core")

    hidden = jnp.maximum(preactivations, jnp.zeros_like(preactivations))
    partial_sum = jnp.dot(hidden, decoder_weight, preferred_element_type=jnp.float32)
    arrived = swap(partial_sum.astype(jnp.bfloat16).reshape(wide, rows, width), "wide")
    mine = arrived.astype(jnp.float32).sum(axis=0).astype(jnp.bfloat16)

    halves = jnp.moveaxis(mine.reshape(rows, cores, half), 1, 0)
    halves = jnp.broadcast_to(halves[None], (pairs, cores, rows, half)).reshape(-1, rows, half)
    block = jnp.broadcast_to(inputs[None], (pairs * cores, rows, columns))
    arrived = swap(jnp.concatenate([halves, block], axis=2), narrow)
    reduced = arrived[:, :, :half].astype(jnp.float32).sum(axis=0)
    whole_rows = jnp.moveaxis(arrived[:, :, half:], 0, 1).reshape(rows, width)
    my_inputs = lax.dynamic_slice_in_dim(whole_rows, core * half, half, 1).astype(jnp.float32)
    my_bias = lax.dynamic_slice_in_dim(decoder_bias, core * half, half)
    residual = (reduced + my_bias - my_inputs).astype(jnp.bfloat16)
    centered = (my_inputs - my_bias).astype(jnp.bfloat16)

    gathered = to_all(jnp.stack([residual, centered]), "wide")
    gathered = jnp.moveaxis(gathered, 0, 1).reshape(2, wide * rows, half)
    both = to_all(gathered, "core")
    residual = jnp.concatenate([both[i, 0] for i in range(cores)], axis=1)
    centered = jnp.concatenate([both[i, 1] for i in range(cores)], axis=1)

    grad_decoder = jnp.einsum(
        "bf,bd->fd", hidden, residual, preferred_element_type=jnp.float32
    ).astype(jnp.bfloat16)
    backward = jnp.einsum("bd,fd->bf", residual, decoder_weight, preferred_element_type=jnp.float32)
    masked = jnp.where(preactivations > 0, backward, jnp.zeros_like(backward)).astype(jnp.bfloat16)
    grad_encoder = jnp.einsum(
        "bd,bf->df", centered, masked, preferred_element_type=jnp.float32
    ).astype(jnp.bfloat16)
    return (grad_encoder, grad_decoder)


def solution(mesh):
    narrow, wide = (mesh.shape[a] for a in ("narrow", "wide"))
    split = Mesh(mesh.devices.reshape(narrow // 2, 2, wide), ("pair", "core", "wide"))
    columns = ("pair", "core")
    features = ("pair", "core", "wide")
    return jax.shard_map(
        shards,
        mesh=split,
        in_specs=(P("wide", columns), P(), P(None, features), P(features, None)),
        out_specs=(P(None, features), P(features, None)),
        check_vma=False,
    )
```

```python
import jax
import jax.numpy as jnp
from jax import lax
from jax.experimental import pallas as pl
from jax.experimental.pallas import tpu as pltpu
from jax.sharding import Mesh, PartitionSpec as P

BF16, F32 = jnp.bfloat16, jnp.float32
LANES = 128


def swap(x, axis):
    return lax.all_to_all(x, axis, split_axis=0, concat_axis=0, tiled=True)


def to_all(x, axis):
    return swap(jnp.broadcast_to(x[None], (lax.axis_size(axis), *x.shape)), axis)


def dot(a, b, contract):
    return lax.dot_general(a, b, ((contract[:1], contract[1:]), ((), ())), preferred_element_type=F32)


def first_kernel(pre, weight, extra, out):
    hidden = jnp.maximum(pre[...], jnp.zeros_like(pre[...]))
    rows = hidden.shape[0]
    out[0, :rows, :] = dot(hidden, weight[...], (1, 0)).astype(BF16)
    out[0, rows:, :] = extra[...]


def first_product(pre, weight, extra):
    rows, features = pre.shape
    half = weight.shape[1] // 2
    more = extra.shape[0]
    return pl.pallas_call(
        first_kernel,
        grid=(2,),
        out_shape=jax.ShapeDtypeStruct((2, rows + more, half), BF16),
        in_specs=[
            pl.BlockSpec((rows, features), lambda i: (0, 0)),
            pl.BlockSpec((features, half), lambda i: (0, i)),
            pl.BlockSpec((more, half), lambda i: (0, 0)),
        ],
        out_specs=pl.BlockSpec((1, rows + more, half), lambda i: (i, 0, 0)),
        name="first_product",
    )(pre, weight, extra)


def last_kernel(both, pre, weight, decoder_out, encoder_out, decoder, encoder, sems):
    cores, rows, _ = both.shape
    features = pre.shape[1]
    half = weight.shape[1] // cores
    hidden = jnp.maximum(pre[...], jnp.zeros_like(pre[...]))
    copies = []

    def send(source, target):
        copies.append(pltpu.make_async_copy(source, target, sems.at[len(copies)]))
        copies[-1].start()

    backward = jnp.zeros((rows, features), F32)
    for c in range(cores):
        residual = both[c, :, :half]
        columns = pl.ds(c * half, half)
        decoder[c] = dot(hidden, residual, (0, 0)).astype(BF16)
        send(decoder.at[c], decoder_out.at[:, columns])
        backward += dot(residual, weight[:, columns], (1, 1))
    masked = jnp.where(pre[...] > 0, backward, jnp.zeros_like(backward)).astype(BF16)
    blocks, width = encoder.shape[:2]
    depth = rows // blocks
    padded = -(-width // LANES) * LANES
    for x in range(blocks):
        part = [
            both[c, x * depth : (x + 1) * depth, half + h * padded : half + (h + 1) * padded]
            for c in range(cores)
            for h in range(blocks // cores)
        ]
        product = dot(jnp.concatenate(part, axis=0), masked, (0, 0))
        encoder[x] = product[:width].astype(BF16)
        send(encoder.at[x], encoder_out.at[pl.ds(x * width, width), :])
    for copy in copies:
        copy.wait()


def last_products(both, pre, weight, blocks):
    cores = both.shape[0]
    features, width = weight.shape
    return pl.pallas_call(
        last_kernel,
        out_shape=(
            jax.ShapeDtypeStruct((features, width), BF16),
            jax.ShapeDtypeStruct((width, features), BF16),
        ),
        in_specs=[pl.BlockSpec(memory_space=pltpu.VMEM)] * 3,
        out_specs=(pl.BlockSpec(memory_space=pl.ANY),) * 2,
        scratch_shapes=[
            pltpu.VMEM((cores, features, width // cores), BF16),
            pltpu.VMEM((blocks, width // blocks, features), BF16),
            pltpu.SemaphoreType.DMA((cores + blocks,)),
        ],
        compiler_params=pltpu.CompilerParams(vmem_limit_bytes=16 << 20),
        name="last_products",
    )(both, pre, weight)


def shards(inputs, decoder_bias, preactivations, decoder_weight):
    rows, columns = inputs.shape
    width = decoder_weight.shape[1]
    xs, yhs, cores, yls, zs = (lax.axis_size(a) for a in ("x", "yh", "core", "yl", "z"))
    x, yh, core, yl, z = (lax.axis_index(a) for a in ("x", "yh", "core", "yl", "z"))
    half, quarter, pair = width // cores, width // xs, columns * cores
    pieces = xs * zs

    extra = jnp.pad(inputs, ((0, 16 - rows), (0, half - columns)))
    arrived = swap(first_product(preactivations, decoder_weight, extra), "core")
    batch = preactivations.shape[0]
    blocks = arrived[:, batch : batch + rows, :columns]
    block = jnp.concatenate([blocks[c] for c in range(cores)], axis=1)
    strip = lax.dynamic_update_slice_in_dim(
        jnp.zeros((rows, half), BF16), block, (x * quarter) % half + yh * pair, 1
    ).astype(F32)
    owner = jnp.where((x * quarter) // half == core, yl * zs + z, pieces)
    whole = arrived[:, :batch].reshape(cores, pieces, rows, half).astype(F32)
    mine = lax.broadcasted_iota(jnp.int32, (pieces, 1, 1), 0) == owner
    partial_sum = whole[0] + whole[1] - jnp.where(mine, strip[None], jnp.zeros_like(strip)[None])

    arrived = swap(partial_sum.astype(BF16), ("x", "z"))
    summed = arrived.astype(F32).sum(axis=0).astype(BF16)
    arrived = to_all(jnp.concatenate([summed, block], axis=1), ("yh", "yl"))
    my_bias = lax.dynamic_slice_in_dim(decoder_bias, core * half, half)
    residual = (arrived[:, :, :half].astype(F32).sum(axis=0) + my_bias).astype(BF16)

    each = yls // cores
    inputs_here = arrived[:, :, half:].reshape(yhs, yls, rows, pair)
    inputs_here = lax.dynamic_slice_in_dim(inputs_here, core * each, each, 1)
    inputs_here = inputs_here.transpose(1, 2, 0, 3).reshape(each, rows, quarter)
    bias_here = lax.dynamic_slice_in_dim(decoder_bias, x * quarter, quarter)
    centered = (inputs_here.astype(F32) - bias_here).astype(BF16)
    spare = -quarter % LANES
    centered = jnp.pad(centered, ((0, 0), (0, 0), (0, spare)))
    payload = jnp.concatenate([residual, *(centered[h] for h in range(each))], axis=1)

    gathered = to_all(payload, ("x", "z")).reshape(batch, -1)
    both = to_all(gathered, "core")
    grad_decoder, grad_encoder = last_products(both, preactivations, decoder_weight, xs)
    return (grad_encoder, grad_decoder)


def solution(mesh):
    split = Mesh(mesh.devices.reshape(4, 2, 2, 4, 8), ("x", "yh", "core", "yl", "z"))
    narrow, wide = ("x", "yh", "core"), ("yl", "z")
    return jax.shard_map(
        shards,
        mesh=split,
        in_specs=(P(wide, narrow), P(), P(None, narrow + wide), P(narrow + wide, None)),
        out_specs=(P(None, narrow + wide), P(narrow + wide, None)),
        check_vma=False,
    )
```

```python
import functools

import jax
import jax.numpy as jnp
from jax import lax
from jax.experimental import pallas as pl
from jax.experimental.pallas import tpu as pltpu
from jax.sharding import Mesh, PartitionSpec as P

BF16, F32 = jnp.bfloat16, jnp.float32
LANES, SUBLANES = 128, 8
EXTRA, CHUNKS = 16, 3
AXES = ("x", "yh", "core", "yl", "z")


def swap(x, axis):
    return lax.all_to_all(x, axis, split_axis=0, concat_axis=0, tiled=True)


def to_all(x, axis):
    return swap(jnp.broadcast_to(x[None], (lax.axis_size(axis), *x.shape)), axis)


def dot(a, b, contract):
    return lax.dot_general(a, b, ((contract[:1], contract[1:]), ((), ())), preferred_element_type=F32)


def first_kernel(pre_hbm, weight_hbm, inputs_hbm, out, pre, weight, inputs, sems):
    cores, _, half = out.shape
    batch = pre.shape[0]
    rows, columns = inputs.shape
    step = half // CHUNKS
    small = [
        pltpu.make_async_copy(pre_hbm, pre, sems.at[0]),
        pltpu.make_async_copy(inputs_hbm, inputs, sems.at[1]),
    ]
    chunks = [pl.ds(i * step, step) for i in range(cores * CHUNKS)]
    large = [
        pltpu.make_async_copy(weight_hbm.at[:, c], weight.at[:, c], sems.at[2 + i])
        for i, c in enumerate(chunks)
    ]
    for copy in small + large:
        copy.start()
    out[:, batch:, :] = jnp.zeros_like(out[:, batch:, :])
    for copy in small:
        copy.wait()
    for c in range(cores):
        out[c, batch : batch + rows, :columns] = inputs[...]
    hidden = jnp.maximum(pre[...], jnp.zeros_like(pre[...]))
    for i, c in enumerate(chunks):
        large[i].wait()
        j = i % CHUNKS
        product = dot(hidden, weight[:, c], (1, 0)).astype(BF16)
        out[i // CHUNKS, :batch, j * step : (j + 1) * step] = product


def first_product(pre, weight, inputs):
    rows = pre.shape[0]
    cores = lax.axis_size("core")
    half = weight.shape[1] // cores
    return pl.pallas_call(
        first_kernel,
        out_shape=jax.ShapeDtypeStruct((cores, rows + EXTRA, half), BF16),
        in_specs=[pl.BlockSpec(memory_space=pltpu.HBM)] * 3,
        out_specs=pl.BlockSpec(memory_space=pltpu.VMEM),
        scratch_shapes=[
            pltpu.VMEM(pre.shape, BF16),
            pltpu.VMEM(weight.shape, BF16),
            pltpu.VMEM(inputs.shape, BF16),
            pltpu.SemaphoreType.DMA((2 + cores * CHUNKS,)),
        ],
        compiler_params=pltpu.CompilerParams(vmem_limit_bytes=66_375_000),
        name="first_product",
    )(pre, weight, inputs)


def second_kernel(rows, columns, arrived, bias, out, block_out, my_bias, total):
    cores, _, half = arrived.shape
    batch = out.shape[0]
    x, yh, core, yl, z = (lax.axis_index(a) for a in AXES)
    own = yl * lax.axis_size("z") + z
    width = half * cores
    quarter = width // lax.axis_size("x")
    tile = arrived[0, batch:, :].astype(F32)
    for c in range(1, cores):
        tile += pltpu.roll(arrived[c, batch:, :].astype(F32), c * columns, 1)
    block_out[...] = tile[:, : block_out.shape[1]].astype(BF16)
    strip = pltpu.roll(tile[:SUBLANES], lax.rem(x * quarter, half) + yh * columns * cores, 1)
    strip = pltpu.roll(strip, lax.rem(own * rows, SUBLANES), 0)
    strip = jnp.where(x * quarter // half == core, strip, jnp.zeros_like(strip))
    total[...] = arrived[0, :batch, :].astype(F32) + arrived[1, :batch, :].astype(F32)
    place = pl.ds(pl.multiple_of(own * rows // SUBLANES * SUBLANES, SUBLANES), SUBLANES)
    total[place, :] -= strip
    out[...] = total[...].astype(BF16)
    whole = bias[...].reshape(1, width)
    my_bias[:, :half] = jnp.where(core == 0, whole[:, :half], whole[:, half:])
    here = pltpu.roll(whole, lax.rem(width - x * quarter, width), 1)[:, : my_bias.shape[1] - half]
    inside = lax.broadcasted_iota(jnp.int32, here.shape, 1) < quarter
    my_bias[:, half:] = jnp.where(inside, here, jnp.zeros_like(here))


def second_sum(arrived, bias, batch, rows, columns):
    _, _, half = arrived.shape
    return pl.pallas_call(
        functools.partial(second_kernel, rows, columns),
        out_shape=(
            jax.ShapeDtypeStruct((batch, half), BF16),
            jax.ShapeDtypeStruct((EXTRA, 3 * LANES), BF16),
            jax.ShapeDtypeStruct((1, half + padded_quarter(bias.shape[0])), F32),
        ),
        in_specs=[pl.BlockSpec(memory_space=pltpu.VMEM)] * 2,
        out_specs=(pl.BlockSpec(memory_space=pltpu.VMEM),) * 3,
        scratch_shapes=[pltpu.VMEM((batch, half), F32)],
        compiler_params=pltpu.CompilerParams(vmem_limit_bytes=8 << 20),
        name="second_sum",
    )(arrived, bias)


def third_kernel(arrived, block, out):
    count, rows, _ = out.shape
    half = arrived.shape[2]
    summed = arrived[...].astype(F32).sum(axis=0).astype(BF16)
    for i in range(count):
        out[i, :, :half] = summed
        out[i, :, half:] = block[:rows, :]


def third_sum(arrived, block, count):
    _, rows, half = arrived.shape
    return pl.pallas_call(
        third_kernel,
        out_shape=jax.ShapeDtypeStruct((count, rows, half + block.shape[1]), BF16),
        in_specs=[pl.BlockSpec(memory_space=pltpu.VMEM)] * 2,
        out_specs=pl.BlockSpec(memory_space=pltpu.VMEM),
        compiler_params=pltpu.CompilerParams(vmem_limit_bytes=8 << 20),
        name="third_sum",
    )(arrived, block)


def padded_quarter(width):
    return -(-(width // lax.axis_size("x")) // LANES) * LANES


def fourth_kernel(half, pair, arrived, bias, out):
    _, rows, _ = arrived.shape
    core = lax.axis_index("core")
    yhs, yls = lax.axis_size("yh"), lax.axis_size("yl")
    each = yls // lax.axis_size("core")
    padded = bias.shape[1] - half
    total = arrived[:, :, :half].astype(F32).sum(axis=0) + bias[:, :half]
    out[:, :half] = total.astype(BF16)
    for h in range(each):
        row = jnp.zeros((rows, padded), F32)
        for yh in range(yhs):
            piece = arrived[yh * yls + core * each + h, :, half:].astype(F32)
            spare = jnp.zeros((rows, padded - piece.shape[1]), F32)
            piece = jnp.concatenate([piece, spare], axis=1)
            row += pltpu.roll(piece, yh * pair, 1) if yh else piece
        place = slice(half + h * padded, half + (h + 1) * padded)
        out[:, place] = (row - bias[:, half:]).astype(BF16)


def fourth_sum(arrived, bias, half, pair):
    _, rows, _ = arrived.shape
    each = lax.axis_size("yl") // lax.axis_size("core")
    padded = bias.shape[1] - half
    return pl.pallas_call(
        functools.partial(fourth_kernel, half, pair),
        out_shape=jax.ShapeDtypeStruct((rows, half + each * padded), BF16),
        in_specs=[pl.BlockSpec(memory_space=pltpu.VMEM)] * 2,
        out_specs=pl.BlockSpec(memory_space=pltpu.VMEM),
        compiler_params=pltpu.CompilerParams(vmem_limit_bytes=8 << 20),
        name="fourth_sum",
    )(arrived, bias)


def last_kernel(both, pre, weight, decoder_out, encoder_out, decoder, encoder, sems):
    cores, rows, _ = both.shape
    features = pre.shape[1]
    half = weight.shape[1] // cores
    hidden = jnp.maximum(pre[...], jnp.zeros_like(pre[...]))
    copies = []

    def send(source, target):
        copies.append(pltpu.make_async_copy(source, target, sems.at[len(copies)]))
        copies[-1].start()

    backward = jnp.zeros((rows, features), F32)
    for c in range(cores):
        residual = both[c, :, :half]
        columns = pl.ds(c * half, half)
        decoder[c] = dot(hidden, residual, (0, 0)).astype(BF16)
        send(decoder.at[c], decoder_out.at[:, columns])
        backward += dot(residual, weight[:, columns], (1, 1))
    masked = jnp.where(pre[...] > 0, backward, jnp.zeros_like(backward)).astype(BF16)
    blocks, width = encoder.shape[:2]
    depth = rows // blocks
    padded = -(-width // LANES) * LANES
    for x in range(blocks):
        part = [
            both[c, x * depth : (x + 1) * depth, half + h * padded : half + (h + 1) * padded]
            for c in range(cores)
            for h in range(blocks // cores)
        ]
        product = dot(jnp.concatenate(part, axis=0), masked, (0, 0))
        encoder[x] = product[:width].astype(BF16)
        send(encoder.at[x], encoder_out.at[pl.ds(x * width, width), :])
    for copy in copies:
        copy.wait()


def last_products(both, pre, weight, blocks):
    cores = both.shape[0]
    features, width = weight.shape
    return pl.pallas_call(
        last_kernel,
        out_shape=(
            jax.ShapeDtypeStruct((features, width), BF16),
            jax.ShapeDtypeStruct((width, features), BF16),
        ),
        in_specs=[pl.BlockSpec(memory_space=pltpu.VMEM)] * 3,
        out_specs=(pl.BlockSpec(memory_space=pl.ANY),) * 2,
        scratch_shapes=[
            pltpu.VMEM((cores, features, width // cores), BF16),
            pltpu.VMEM((blocks, width // blocks, features), BF16),
            pltpu.SemaphoreType.DMA((cores + blocks,)),
        ],
        compiler_params=pltpu.CompilerParams(vmem_limit_bytes=16 << 20),
        name="last_products",
    )(both, pre, weight)


def shards(inputs, decoder_bias, preactivations, decoder_weight):
    rows, columns = inputs.shape
    batch = preactivations.shape[0]
    half = decoder_weight.shape[1] // lax.axis_size("core")
    pieces = lax.axis_size(("x", "z"))

    arrived = swap(first_product(preactivations, decoder_weight, inputs), "core")
    partial_sum, block, bias = second_sum(arrived, decoder_bias, batch, rows, columns)
    arrived = swap(partial_sum.reshape(pieces, rows, half), ("x", "z"))
    payload = third_sum(arrived, block, lax.axis_size(("yh", "yl")))
    arrived = swap(payload, ("yh", "yl"))
    payload = fourth_sum(arrived, bias, half, columns * lax.axis_size("core"))
    gathered = to_all(payload, ("x", "z")).reshape(batch, -1)
    both = to_all(gathered, "core")
    grad_decoder, grad_encoder = last_products(
        both, preactivations, decoder_weight, lax.axis_size("x")
    )
    return (grad_encoder, grad_decoder)


def solution(mesh):
    split = Mesh(mesh.devices.reshape(4, 2, 2, 4, 8), AXES)
    narrow, wide = ("x", "yh", "core"), ("yl", "z")
    return jax.shard_map(
        shards,
        mesh=split,
        in_specs=(P(wide, narrow), P(), P(None, narrow + wide), P(narrow + wide, None)),
        out_specs=(P(None, narrow + wide), P(narrow + wide, None)),
        check_vma=False,
    )
```

```python
import functools

import jax
import jax.numpy as jnp
from jax import lax
from jax.experimental import pallas as pl
from jax.experimental.pallas import tpu as pltpu
from jax.sharding import Mesh, PartitionSpec as P

BF16, F32 = jnp.bfloat16, jnp.float32
LANES, SUBLANES, CHUNKS = 128, 8, 3
AXES = ("x", "yh", "core", "ya", "yb", "za", "zb")
SIZES = (4, 2, 2, 2, 2, 4, 2)
NEAR, FAR = ("x", "yb", "zb"), ("yh", "ya", "za")
VMEM = pl.BlockSpec(memory_space=pltpu.VMEM)


def swap(x, axis):
    return lax.all_to_all(x, axis, split_axis=0, concat_axis=0, tiled=True)


def dot(a, b, contract):
    return lax.dot_general(a, b, ((contract[:1], contract[1:]), ((), ())), preferred_element_type=F32)


def small_kernel(kernel, result, limit, name, *operands):
    return pl.pallas_call(
        kernel,
        out_shape=result,
        in_specs=[VMEM] * len(operands),
        out_specs=VMEM,
        compiler_params=pltpu.CompilerParams(vmem_limit_bytes=limit << 20),
        name=name,
    )(*operands)


def row_order(batch, rows):
    shape = (batch, batch)
    new = lax.broadcasted_iota(jnp.int32, shape, 0)
    group, r = new // rows, lax.rem(new, rows)
    ya, group = lax.rem(group, 2), group // 2
    zb, group = lax.rem(group, 2), group // 2
    yb, za = lax.rem(group, 2), group // 2
    old = ((((ya * 2 + yb) * 4 + za) * 2) + zb) * rows + r
    return jnp.where(lax.broadcasted_iota(jnp.int32, shape, 1) == old, 1.0, 0.0).astype(BF16)


def first_kernel(
    pre_hbm, weight_hbm, inputs_hbm, bias_hbm, out, ordered, tile, pre, weight, inputs, bias, sems
):
    count, piece, half = out.shape
    batch, width = pre.shape[0], weight.shape[1]
    rows, columns = inputs.shape
    tiles = batch // piece
    step = half // CHUNKS
    chunks = [pl.ds(i * step, step) for i in range(width // step)]
    pairs = [(inputs_hbm, inputs), (bias_hbm, bias), (pre_hbm, pre)]
    pairs += [(weight_hbm.at[:, c], weight.at[:, c]) for c in chunks]
    copies = [pltpu.make_async_copy(a, b, sems.at[i]) for i, (a, b) in enumerate(pairs)]
    for copy in copies:
        copy.start()
    order = row_order(batch, rows)
    x, yh, core, ya, yb, za, zb = (lax.axis_index(a) for a in AXES)
    first = ((x * 2 + yh) * 2 + core) * columns
    copies[0].wait()
    copies[1].wait()
    whole = bias[...].reshape(1, width)
    here = pltpu.roll(whole, lax.rem(width - first, width), 1)[:, :columns]
    mine = inputs[...].astype(F32) - here
    spare = jnp.zeros((rows, 2 * LANES - columns), F32)
    padded = jnp.concatenate([mine, spare], axis=1)
    tile[...] = jnp.concatenate([padded[:, :LANES], padded[:, LANES:]], axis=0).astype(BF16)
    strip = jnp.concatenate([mine, jnp.zeros((rows, width - columns), F32)], axis=1)
    strip = jnp.concatenate([strip, jnp.zeros((piece - rows, width), F32)], axis=0)
    strip = pltpu.roll(pltpu.roll(strip, first, 1), ya * rows, 0)
    place = (za * 2 + yb) * 2 + zb
    copies[2].wait()
    ordered[...] = dot(order, pre[...], (1, 0)).astype(BF16)
    hidden = jnp.maximum(ordered[...], jnp.zeros_like(ordered[...]))
    for i, c in enumerate(chunks):
        copies[3 + i].wait()
        product = dot(hidden, weight[:, c], (1, 0)).reshape(tiles, piece, step)
        part = strip[:, i * step : (i + 1) * step]
        owned = lax.broadcasted_iota(jnp.int32, product.shape, 0) == place
        product = product - jnp.where(owned, part[None], jnp.zeros_like(part)[None])
        core_there, j = i // CHUNKS, i % CHUNKS
        out[core_there * tiles : (core_there + 1) * tiles, :, j * step : (j + 1) * step] = (
            product.astype(BF16)
        )


def first_product(pre, weight, inputs, bias):
    cores = lax.axis_size("core")
    near = lax.axis_size(NEAR)
    operands = (pre, weight, inputs, bias)
    return pl.pallas_call(
        first_kernel,
        out_shape=(
            pltpu.VMEM((cores * near, pre.shape[0] // near, weight.shape[1] // cores), BF16),
            pltpu.VMEM(pre.shape, BF16),
            pltpu.VMEM((SUBLANES, LANES), BF16),
        ),
        in_specs=[pl.BlockSpec(memory_space=pltpu.HBM)] * 4,
        out_specs=(VMEM,) * 3,
        scratch_shapes=[pltpu.VMEM(a.shape, a.dtype) for a in operands]
        + [pltpu.SemaphoreType.DMA((3 + cores * CHUNKS,))],
        compiler_params=pltpu.CompilerParams(vmem_limit_bytes=12 << 20),
        name="first_product",
    )(*(pltpu.with_memory_space_constraint(a, pltpu.HBM) for a in operands))


def second_kernel(arrived, tile, out):
    half = arrived.shape[2]
    summed = arrived[...].astype(F32).sum(axis=0).astype(BF16)
    for i in range(out.shape[0]):
        out[i, :, :half] = summed
        out[i, :, half:] = tile[...]


def third_kernel(half, tail, arrived, out):
    yhs, yas, zas = (lax.axis_size(a) for a in FAR)
    piece = arrived.shape[1]
    total = arrived[:, :, :half].astype(F32).sum(axis=0).astype(BF16)
    upper = lax.broadcasted_iota(jnp.int32, (piece, LANES), 0) < piece // yas
    parts, tails = [total], jnp.zeros((piece, LANES), F32)
    for za in range(zas):
        for yh in range(yhs):
            low, high = (
                arrived[(yh * yas + ya) * zas + za, :, half:].astype(F32) for ya in range(yas)
            )
            parts.append(jnp.where(upper, low, pltpu.roll(high, piece // yas, 0)).astype(BF16))
            rest = jnp.where(upper, pltpu.roll(low, piece // yas, 0), high)
            shift = (za * yhs + yh) * tail
            tails += pltpu.roll(rest, shift, 1) if shift else rest
    parts.append(tails.astype(BF16))
    payload = jnp.concatenate(parts, axis=1)
    for i in range(out.shape[0]):
        out[i] = payload


def last_kernel(tail, own, other, pre, weight, decoder_out, encoder_out, decoder, encoder, sems):
    batch, _ = own.shape
    core = lax.axis_index("core")
    cores, xs, yhs, zas = (lax.axis_size(a) for a in ("core", "x", "yh", "za"))
    half = weight.shape[1] // cores
    depth, span = batch // zas, LANES + tail
    sources = ((own, core), (other, 1 - core))
    hidden = jnp.maximum(pre[...], jnp.zeros_like(pre[...]))
    copies = []

    def send(source, target):
        copies.append(pltpu.make_async_copy(source, target, sems.at[len(copies)]))
        copies[-1].start()

    backward = jnp.zeros(pre.shape, F32)
    for k, (source, c) in enumerate(sources):
        residual = source[:, :half]
        columns = pl.ds(pl.multiple_of(c * half, LANES), half)
        decoder[k] = dot(hidden, residual, (0, 0)).astype(BF16)
        send(decoder.at[k], decoder_out.at[:, columns])
        backward += dot(residual, weight[:, columns], (1, 1))
    masked = jnp.where(pre[...] > 0, backward, jnp.zeros_like(backward)).astype(BF16)

    lane = lax.broadcasted_iota(jnp.int32, (depth, LANES), 1) // (yhs * tail)
    ends = []
    for source, _ in sources:
        pieces = [
            source[x * depth : (x + 1) * depth, half + zas * yhs * LANES :].astype(F32)
            for x in range(xs)
        ]
        blocks = []
        for za in range(zas):
            block = jnp.zeros((depth, LANES), F32)
            for x in range(xs):
                shift = (x - za) * yhs * tail % LANES
                moved = pltpu.roll(pieces[x], shift, 1) if shift else pieces[x]
                block = jnp.where(lane == x, moved, block)
            blocks.append(block.astype(BF16))
        ends.append(dot(jnp.concatenate(blocks, axis=0), masked, (0, 0)).astype(BF16))

    for x in range(xs):
        for k, (source, c) in enumerate(sources):
            size = yhs * LANES
            part = [
                source[x * depth : (x + 1) * depth, half + za * size : half + (za + 1) * size]
                for za in range(zas)
            ]
            product = dot(jnp.concatenate(part, axis=0), masked, (0, 0)).astype(BF16)
            for yh in range(yhs):
                start = pl.multiple_of(((x * yhs + yh) * cores + c) * span, tail)
                encoder[pl.ds(start, LANES), :] = product[yh * LANES : (yh + 1) * LANES]
                end = (x * yhs + yh) * tail
                encoder[pl.ds(pl.multiple_of(start + LANES, tail), tail), :] = ends[k][end : end + tail]
        block = pl.ds(x * yhs * cores * span, yhs * cores * span)
        send(encoder.at[block], encoder_out.at[block])
    for copy in copies:
        copy.wait()


def last_products(own, other, pre, weight, tail):
    cores = lax.axis_size("core")
    features, width = weight.shape
    return pl.pallas_call(
        functools.partial(last_kernel, tail),
        out_shape=(
            jax.ShapeDtypeStruct((features, width), BF16),
            jax.ShapeDtypeStruct((width, features), BF16),
        ),
        in_specs=[VMEM] * 4,
        out_specs=(pl.BlockSpec(memory_space=pl.ANY),) * 2,
        scratch_shapes=[
            pltpu.VMEM((cores, features, width // cores), BF16),
            pltpu.VMEM((width, features), BF16),
            pltpu.SemaphoreType.DMA((cores + lax.axis_size("x"),)),
        ],
        compiler_params=pltpu.CompilerParams(vmem_limit_bytes=20 << 20),
        name="last_products",
    )(own, other, pre, weight)


def shards(inputs, decoder_bias, preactivations, decoder_weight):
    columns = inputs.shape[1]
    batch, width = preactivations.shape[0], decoder_weight.shape[1]
    half = width // lax.axis_size("core")
    tail = columns - LANES
    near, far = lax.axis_size(NEAR), lax.axis_size(FAR)
    piece = batch // near

    pieces, ordered, tile = first_product(preactivations, decoder_weight, inputs, decoder_bias)
    arrived = swap(pieces, ("core", *NEAR))
    shape = jax.ShapeDtypeStruct((far, piece, half + LANES), BF16)
    arrived = swap(small_kernel(second_kernel, shape, 8, "second_sum", arrived, tile), FAR)
    shape = jax.ShapeDtypeStruct((near, piece, width), BF16)
    kernel = functools.partial(third_kernel, half, tail)
    own = swap(small_kernel(kernel, shape, 8, "third_sum", arrived), NEAR).reshape(batch, width)
    other = lax.ppermute(own, "core", [(0, 1), (1, 0)])
    grad_decoder, grad_encoder = last_products(own, other, ordered, decoder_weight, tail)
    return (grad_encoder, grad_decoder)


def solution(mesh):
    split = Mesh(mesh.devices.reshape(SIZES), AXES)
    narrow, wide = AXES[:3], AXES[3:]
    return jax.shard_map(
        shards,
        mesh=split,
        in_specs=(P(wide, narrow), P(), P(None, narrow + wide), P(narrow + wide, None)),
        out_specs=(P(None, narrow + wide), P(narrow + wide, None)),
        check_vma=False,
    )
```

```python
import functools

import jax
import jax.numpy as jnp
from jax import lax
from jax.experimental import pallas as pl
from jax.experimental.pallas import tpu as pltpu
from jax.sharding import Mesh, PartitionSpec as P

BF16, F32 = jnp.bfloat16, jnp.float32
LANES, SUBLANES, CHUNKS = 128, 8, 3
AXES = ("x", "yh", "core", "ya", "yb", "za", "zb")
SIZES = (4, 2, 2, 2, 2, 4, 2)
NEAR, FAR = ("x", "yb", "zb"), ("yh", "ya", "za")
VMEM = pl.BlockSpec(memory_space=pltpu.VMEM)


def swap(x, axis):
    return lax.all_to_all(x, axis, split_axis=0, concat_axis=0, tiled=True)


def dot(a, b, contract):
    return lax.dot_general(a, b, ((contract[:1], contract[1:]), ((), ())), preferred_element_type=F32)


def small_kernel(kernel, result, limit, name, *operands):
    return pl.pallas_call(
        kernel,
        out_shape=result,
        in_specs=[VMEM] * len(operands),
        out_specs=VMEM,
        compiler_params=pltpu.CompilerParams(vmem_limit_bytes=limit << 20),
        name=name,
    )(*operands)


def row_order(batch, rows):
    shape = (batch, batch)
    new = lax.broadcasted_iota(jnp.int32, shape, 0)
    group, r = new // rows, lax.rem(new, rows)
    ya, group = lax.rem(group, 2), group // 2
    zb, group = lax.rem(group, 2), group // 2
    yb, za = lax.rem(group, 2), group // 2
    old = ((((ya * 2 + yb) * 4 + za) * 2) + zb) * rows + r
    return jnp.where(lax.broadcasted_iota(jnp.int32, shape, 1) == old, 1.0, 0.0).astype(BF16)


def first_kernel(
    pre_hbm, weight_hbm, inputs_hbm, bias_hbm, out, ordered, tile, strip, pre, weight, inputs, bias, sems
):
    batch, half = out.shape
    piece, width = strip.shape[0], bias.shape[0]
    rows, columns = inputs.shape
    step = half // CHUNKS
    x, yh, core, ya, yb, za, zb = (lax.axis_index(a) for a in AXES)
    there = (1 - core) * half
    pairs = [(inputs_hbm, inputs), (bias_hbm, bias), (pre_hbm, pre)]
    for i in range(CHUNKS):
        columns_there = pl.ds(pl.multiple_of(there + i * step, LANES), step)
        pairs.append((weight_hbm.at[:, columns_there], weight.at[:, pl.ds(i * step, step)]))
    copies = [pltpu.make_async_copy(a, b, sems.at[i]) for i, (a, b) in enumerate(pairs)]
    for copy in copies:
        copy.start()
    order = row_order(batch, rows)
    first = ((x * 2 + yh) * 2 + core) * columns
    copies[0].wait()
    copies[1].wait()
    whole = bias[...].reshape(1, width)
    here = pltpu.roll(whole, lax.rem(width - first, width), 1)[:, :columns]
    mine = inputs[...].astype(F32) - here
    spare = jnp.zeros((rows, 2 * LANES - columns), F32)
    padded = jnp.concatenate([mine, spare], axis=1)
    tile[...] = jnp.concatenate([padded[:, :LANES], padded[:, LANES:]], axis=0).astype(BF16)
    line = jnp.concatenate([mine, jnp.zeros((rows, half - columns), F32)], axis=1)
    line = jnp.concatenate([line, jnp.zeros((piece - rows, half), F32)], axis=0)
    strip[...] = pltpu.roll(pltpu.roll(line, lax.rem(first, half), 1), ya * rows, 0)
    copies[2].wait()
    ordered[...] = dot(order, pre[...], (1, 0)).astype(BF16)
    hidden = jnp.maximum(ordered[...], jnp.zeros_like(ordered[...]))
    place = jnp.where(first // half == core, batch, (za * 2 + yb) * 2 + zb)
    for i in range(CHUNKS):
        copies[3 + i].wait()
        part = pl.ds(i * step, step)
        product = dot(hidden, weight[:, part], (1, 0))
        out[:, part] = less(product, strip[:, part], place).astype(BF16)


def less(product, strip, place):
    piece = strip.shape[0]
    pieces = product.reshape(product.shape[0] // piece, *strip.shape)
    owned = lax.broadcasted_iota(jnp.int32, pieces.shape, 0) == place
    pieces = pieces - jnp.where(owned, strip[None], jnp.zeros_like(strip)[None])
    return pieces.reshape(product.shape)


def first_product(pre, weight, inputs, bias):
    half = weight.shape[1] // lax.axis_size("core")
    operands = (pre, weight, inputs, bias)
    return pl.pallas_call(
        first_kernel,
        out_shape=(
            pltpu.VMEM((pre.shape[0], half), BF16),
            pltpu.VMEM(pre.shape, BF16),
            pltpu.VMEM((SUBLANES, LANES), BF16),
            pltpu.VMEM((SUBLANES, half), F32),
        ),
        in_specs=[pl.BlockSpec(memory_space=pltpu.HBM)] * 4,
        out_specs=(VMEM,) * 4,
        scratch_shapes=[
            pltpu.VMEM(pre.shape, BF16),
            pltpu.VMEM((weight.shape[0], half), BF16),
            pltpu.VMEM(inputs.shape, BF16),
            pltpu.VMEM(bias.shape, F32),
            pltpu.SemaphoreType.DMA((3 + CHUNKS,)),
        ],
        compiler_params=pltpu.CompilerParams(vmem_limit_bytes=12 << 20),
        name="first_product",
    )(*(pltpu.with_memory_space_constraint(a, pltpu.HBM) for a in operands))


def own_kernel(ordered, strip, weight_hbm, out, weight, sems):
    batch, half = out.shape
    step = half // CHUNKS
    x, yh, core, ya, yb, za, zb = (lax.axis_index(a) for a in AXES)
    copies = []
    for i in range(CHUNKS):
        columns = pl.ds(pl.multiple_of(core * half + i * step, LANES), step)
        target = weight.at[:, pl.ds(i * step, step)]
        copies.append(pltpu.make_async_copy(weight_hbm.at[:, columns], target, sems.at[i]))
        copies[-1].start()
    hidden = jnp.maximum(ordered[...], jnp.zeros_like(ordered[...]))
    place = jnp.where(x * 2 // lax.axis_size("x") == core, (za * 2 + yb) * 2 + zb, batch)
    for i in range(CHUNKS):
        copies[i].wait()
        part = pl.ds(i * step, step)
        product = dot(hidden, weight[:, part], (1, 0))
        out[:, part] = less(product, strip[:, part], place)


def own_product(ordered, strip, weight):
    batch, features = ordered.shape
    half = strip.shape[1]
    return pl.pallas_call(
        own_kernel,
        out_shape=pltpu.VMEM((batch, half), F32),
        in_specs=[VMEM, VMEM, pl.BlockSpec(memory_space=pltpu.HBM)],
        out_specs=VMEM,
        scratch_shapes=[
            pltpu.VMEM((features, half), BF16),
            pltpu.SemaphoreType.DMA((CHUNKS,)),
        ],
        compiler_params=pltpu.CompilerParams(vmem_limit_bytes=8 << 20),
        cost_estimate=pl.CostEstimate(
            flops=2 * batch * features * half, bytes_accessed=features * half * 2, transcendentals=0
        ),
        name="own_product",
    )(ordered, strip, pltpu.with_memory_space_constraint(weight, pltpu.HBM))


def join_kernel(own, arrived, out):
    out[...] = (own[...] + arrived[...].astype(F32)).reshape(out.shape).astype(BF16)


def second_kernel(arrived, tile, out):
    half = arrived.shape[2]
    summed = arrived[...].astype(F32).sum(axis=0).astype(BF16)
    for i in range(out.shape[0]):
        out[i, :, :half] = summed
        out[i, :, half:] = tile[...]


def third_kernel(half, tail, arrived, out):
    yhs, yas, zas = (lax.axis_size(a) for a in FAR)
    piece = arrived.shape[1]
    total = arrived[:, :, :half].astype(F32).sum(axis=0).astype(BF16)
    upper = lax.broadcasted_iota(jnp.int32, (piece, LANES), 0) < piece // yas
    parts, tails = [total], jnp.zeros((piece, LANES), F32)
    for za in range(zas):
        for yh in range(yhs):
            low, high = (
                arrived[(yh * yas + ya) * zas + za, :, half:].astype(F32) for ya in range(yas)
            )
            parts.append(jnp.where(upper, low, pltpu.roll(high, piece // yas, 0)).astype(BF16))
            rest = jnp.where(upper, pltpu.roll(low, piece // yas, 0), high)
            shift = (za * yhs + yh) * tail
            tails += pltpu.roll(rest, shift, 1) if shift else rest
    parts.append(tails.astype(BF16))
    payload = jnp.concatenate(parts, axis=1)
    for i in range(out.shape[0]):
        out[i] = payload


def near_kernel(own, pre, weight, decoder_out, backward, decoder, sem):
    half = decoder.shape[1]
    core = lax.axis_index("core")
    hidden = jnp.maximum(pre[...], jnp.zeros_like(pre[...]))
    columns = pl.ds(pl.multiple_of(core * half, LANES), half)
    decoder[...] = dot(hidden, own[:, :half], (0, 0)).astype(BF16)
    copy = pltpu.make_async_copy(decoder, decoder_out.at[:, columns], sem)
    copy.start()
    backward[...] = dot(own[:, :half], weight[:, columns], (1, 1))
    copy.wait()


def near_products(own, pre, weight):
    features, width = weight.shape
    half = width // lax.axis_size("core")
    return pl.pallas_call(
        near_kernel,
        out_shape=(pltpu.HBM((features, width), BF16), pltpu.VMEM(pre.shape, F32)),
        in_specs=[VMEM] * 3,
        out_specs=(pl.BlockSpec(memory_space=pltpu.HBM), VMEM),
        scratch_shapes=[pltpu.VMEM((features, half), BF16), pltpu.SemaphoreType.DMA],
        compiler_params=pltpu.CompilerParams(vmem_limit_bytes=10 << 20),
        cost_estimate=pl.CostEstimate(
            flops=4 * pre.shape[0] * features * half,
            bytes_accessed=features * width * 2,
            transcendentals=0,
        ),
        name="near_products",
    )(own, pre, weight)


def last_kernel(
    tail, own, other, pre, weight, backward, _, decoder_out, encoder_out, decoder, encoder, sems
):
    batch, half = other.shape[0], decoder.shape[1]
    core = lax.axis_index("core")
    cores, xs, yhs, zas = (lax.axis_size(a) for a in ("core", "x", "yh", "za"))
    depth, span = batch // zas, LANES + tail
    sources = ((own, core), (other, 1 - core))
    copies = []

    def send(source, target):
        copies.append(pltpu.make_async_copy(source, target, sems.at[len(copies)]))
        copies[-1].start()

    columns = pl.ds(pl.multiple_of((1 - core) * half, LANES), half)
    residual = other[:, :half]
    total = backward[...] + dot(residual, weight[:, columns], (1, 1))
    masked = jnp.where(pre[...] > 0, total, jnp.zeros_like(total)).astype(BF16)
    hidden = jnp.maximum(pre[...], jnp.zeros_like(pre[...]))
    decoder[...] = dot(hidden, residual, (0, 0)).astype(BF16)
    send(decoder, decoder_out.at[:, columns])

    lane = lax.broadcasted_iota(jnp.int32, (depth, LANES), 1) // (yhs * tail)
    ends = []
    for source, _ in sources:
        pieces = [
            source[x * depth : (x + 1) * depth, half + zas * yhs * LANES :].astype(F32)
            for x in range(xs)
        ]
        blocks = []
        for za in range(zas):
            block = jnp.zeros((depth, LANES), F32)
            for x in range(xs):
                shift = (x - za) * yhs * tail % LANES
                moved = pltpu.roll(pieces[x], shift, 1) if shift else pieces[x]
                block = jnp.where(lane == x, moved, block)
            blocks.append(block.astype(BF16))
        ends.append(dot(jnp.concatenate(blocks, axis=0), masked, (0, 0)).astype(BF16))

    for x in range(xs):
        for k, (source, c) in enumerate(sources):
            size = yhs * LANES
            part = [
                source[x * depth : (x + 1) * depth, half + za * size : half + (za + 1) * size]
                for za in range(zas)
            ]
            product = dot(jnp.concatenate(part, axis=0), masked, (0, 0)).astype(BF16)
            for yh in range(yhs):
                start = pl.multiple_of(((x * yhs + yh) * cores + c) * span, tail)
                encoder[pl.ds(start, LANES), :] = product[yh * LANES : (yh + 1) * LANES]
                end = (x * yhs + yh) * tail
                encoder[pl.ds(pl.multiple_of(start + LANES, tail), tail), :] = ends[k][end : end + tail]
        block = pl.ds(x * yhs * cores * span, yhs * cores * span)
        send(encoder.at[block], encoder_out.at[block])
    for copy in copies:
        copy.wait()


def last_products(own, other, pre, weight, backward, decoder, tail):
    features, width = weight.shape
    raw = pl.BlockSpec(memory_space=pltpu.HBM)
    return pl.pallas_call(
        functools.partial(last_kernel, tail),
        out_shape=(
            jax.ShapeDtypeStruct((features, width), BF16),
            jax.ShapeDtypeStruct((width, features), BF16),
        ),
        in_specs=[VMEM] * 5 + [raw],
        out_specs=(raw, raw),
        scratch_shapes=[
            pltpu.VMEM((features, width // lax.axis_size("core")), BF16),
            pltpu.VMEM((width, features), BF16),
            pltpu.SemaphoreType.DMA((1 + lax.axis_size("x"),)),
        ],
        input_output_aliases={5: 0},
        compiler_params=pltpu.CompilerParams(vmem_limit_bytes=20 << 20),
        name="last_products",
    )(own, other, pre, weight, backward, decoder)


def shards(inputs, decoder_bias, preactivations, decoder_weight):
    columns = inputs.shape[1]
    batch, width = preactivations.shape[0], decoder_weight.shape[1]
    half = width // lax.axis_size("core")
    tail = columns - LANES
    near, far = lax.axis_size(NEAR), lax.axis_size(FAR)
    piece = batch // near
    partner = [(0, 1), (1, 0)]

    theirs, ordered, tile, strip = first_product(
        preactivations, decoder_weight, inputs, decoder_bias
    )
    arrived = lax.ppermute(theirs, "core", partner)
    mine = own_product(ordered, strip, decoder_weight)
    shape = jax.ShapeDtypeStruct((near, piece, half), BF16)
    arrived = swap(small_kernel(join_kernel, shape, 8, "join_cores", mine, arrived), NEAR)
    shape = jax.ShapeDtypeStruct((far, piece, half + LANES), BF16)
    arrived = swap(small_kernel(second_kernel, shape, 8, "second_sum", arrived, tile), FAR)
    shape = jax.ShapeDtypeStruct((near, piece, width), BF16)
    kernel = functools.partial(third_kernel, half, tail)
    own = swap(small_kernel(kernel, shape, 8, "third_sum", arrived), NEAR).reshape(batch, width)
    other = lax.ppermute(own, "core", partner)
    decoder, backward = near_products(own, ordered, decoder_weight)
    grad_decoder, grad_encoder = last_products(
        own, other, ordered, decoder_weight, backward, decoder, tail
    )
    return (grad_encoder, grad_decoder)


def solution(mesh):
    split = Mesh(mesh.devices.reshape(SIZES), AXES)
    narrow, wide = AXES[:3], AXES[3:]
    return jax.shard_map(
        shards,
        mesh=split,
        in_specs=(P(wide, narrow), P(), P(None, narrow + wide), P(narrow + wide, None)),
        out_specs=(P(None, narrow + wide), P(narrow + wide, None)),
        check_vma=False,
    )
```

```python
import functools

import jax
import jax.numpy as jnp
from jax import lax
from jax.experimental import pallas as pl
from jax.experimental.pallas import tpu as pltpu
from jax.sharding import Mesh, PartitionSpec as P

BF16, F32 = jnp.bfloat16, jnp.float32
LANES, SUBLANES, CHUNKS = 128, 8, 3
AXES = ("x", "yh", "core", "ya", "yb", "za", "zb")
SIZES = (4, 2, 2, 2, 2, 4, 2)
NEAR, FAR = ("x", "yb", "zb"), ("yh", "ya", "za")
VMEM = pl.BlockSpec(memory_space=pltpu.VMEM)


def swap(x, axis):
    return lax.all_to_all(x, axis, split_axis=0, concat_axis=0, tiled=True)


def dot(a, b, contract):
    return lax.dot_general(a, b, ((contract[:1], contract[1:]), ((), ())), preferred_element_type=F32)


def small_kernel(kernel, result, limit, name, *operands):
    return pl.pallas_call(
        kernel,
        out_shape=result,
        in_specs=[VMEM] * len(operands),
        out_specs=VMEM,
        compiler_params=pltpu.CompilerParams(vmem_limit_bytes=limit << 20),
        name=name,
    )(*operands)


def row_order(batch, rows):
    shape = (batch, batch)
    new = lax.broadcasted_iota(jnp.int32, shape, 0)
    group, r = new // rows, lax.rem(new, rows)
    ya, group = lax.rem(group, 2), group // 2
    zb, group = lax.rem(group, 2), group // 2
    yb, za = lax.rem(group, 2), group // 2
    old = ((((ya * 2 + yb) * 4 + za) * 2) + zb) * rows + r
    return jnp.where(lax.broadcasted_iota(jnp.int32, shape, 1) == old, 1.0, 0.0).astype(BF16)


def first_kernel(
    pre_hbm, weight_hbm, inputs_hbm, bias_hbm, out, ordered, tile, strip, pre, weight, inputs, bias, sems
):
    batch, half = out.shape
    piece, width = strip.shape[0], bias.shape[0]
    rows, columns = inputs.shape
    step = half // CHUNKS
    x, yh, core, ya, yb, za, zb = (lax.axis_index(a) for a in AXES)
    there = (1 - core) * half
    pairs = [(inputs_hbm, inputs), (bias_hbm, bias), (pre_hbm, pre)]
    for i in range(CHUNKS):
        columns_there = pl.ds(pl.multiple_of(there + i * step, LANES), step)
        pairs.append((weight_hbm.at[:, columns_there], weight.at[:, pl.ds(i * step, step)]))
    copies = [pltpu.make_async_copy(a, b, sems.at[i]) for i, (a, b) in enumerate(pairs)]
    for copy in copies[2:] + copies[:2]:
        copy.start()
    order = row_order(batch, rows)
    first = ((x * 2 + yh) * 2 + core) * columns
    copies[2].wait()
    ordered[...] = dot(order, pre[...], (1, 0)).astype(BF16)
    hidden = jnp.maximum(ordered[...], jnp.zeros_like(ordered[...]))
    copies[0].wait()
    copies[1].wait()
    whole = bias[...].reshape(1, width)
    here = pltpu.roll(whole, lax.rem(width - first, width), 1)[:, :columns]
    mine = inputs[...].astype(F32) - here
    spare = jnp.zeros((rows, 2 * LANES - columns), F32)
    padded = jnp.concatenate([mine, spare], axis=1)
    tile[...] = jnp.concatenate([padded[:, :LANES], padded[:, LANES:]], axis=0).astype(BF16)
    line = jnp.concatenate([mine, jnp.zeros((rows, half - columns), F32)], axis=1)
    line = jnp.concatenate([line, jnp.zeros((piece - rows, half), F32)], axis=0)
    strip[...] = pltpu.roll(pltpu.roll(line, lax.rem(first, half), 1), ya * rows, 0)
    place = jnp.where(first // half == core, batch, (za * 2 + yb) * 2 + zb)
    for i in range(CHUNKS):
        copies[3 + i].wait()
        part = pl.ds(i * step, step)
        product = dot(hidden, weight[:, part], (1, 0))
        out[:, part] = less(product, strip[:, part], place).astype(BF16)


def less(product, strip, place):
    piece = strip.shape[0]
    pieces = product.reshape(product.shape[0] // piece, *strip.shape)
    owned = lax.broadcasted_iota(jnp.int32, pieces.shape, 0) == place
    pieces = pieces - jnp.where(owned, strip[None], jnp.zeros_like(strip)[None])
    return pieces.reshape(product.shape)


def first_product(pre, weight, inputs, bias):
    half = weight.shape[1] // lax.axis_size("core")
    operands = (pre, weight, inputs, bias)
    return pl.pallas_call(
        first_kernel,
        out_shape=(
            pltpu.VMEM((pre.shape[0], half), BF16),
            pltpu.VMEM(pre.shape, BF16),
            pltpu.VMEM((SUBLANES, LANES), BF16),
            pltpu.VMEM((SUBLANES, half), F32),
        ),
        in_specs=[pl.BlockSpec(memory_space=pltpu.HBM)] * 4,
        out_specs=(VMEM,) * 4,
        scratch_shapes=[
            pltpu.VMEM(pre.shape, BF16),
            pltpu.VMEM((weight.shape[0], half), BF16),
            pltpu.VMEM(inputs.shape, BF16),
            pltpu.VMEM(bias.shape, F32),
            pltpu.SemaphoreType.DMA((3 + CHUNKS,)),
        ],
        compiler_params=pltpu.CompilerParams(vmem_limit_bytes=12 << 20),
        name="first_product",
    )(*(pltpu.with_memory_space_constraint(a, pltpu.HBM) for a in operands))


def own_kernel(ordered, strip, weight_hbm, out, weight, sems):
    batch, half = out.shape
    step = half // CHUNKS
    x, yh, core, ya, yb, za, zb = (lax.axis_index(a) for a in AXES)
    copies = []
    for i in range(CHUNKS):
        columns = pl.ds(pl.multiple_of(core * half + i * step, LANES), step)
        target = weight.at[:, pl.ds(i * step, step)]
        copies.append(pltpu.make_async_copy(weight_hbm.at[:, columns], target, sems.at[i]))
        copies[-1].start()
    hidden = jnp.maximum(ordered[...], jnp.zeros_like(ordered[...]))
    place = jnp.where(x * 2 // lax.axis_size("x") == core, (za * 2 + yb) * 2 + zb, batch)
    for i in range(CHUNKS):
        copies[i].wait()
        part = pl.ds(i * step, step)
        product = dot(hidden, weight[:, part], (1, 0))
        out[:, part] = less(product, strip[:, part], place)


def own_product(ordered, strip, weight):
    batch, features = ordered.shape
    half = strip.shape[1]
    return pl.pallas_call(
        own_kernel,
        out_shape=pltpu.VMEM((batch, half), F32),
        in_specs=[VMEM, VMEM, pl.BlockSpec(memory_space=pltpu.HBM)],
        out_specs=VMEM,
        scratch_shapes=[
            pltpu.VMEM((features, half), BF16),
            pltpu.SemaphoreType.DMA((CHUNKS,)),
        ],
        compiler_params=pltpu.CompilerParams(vmem_limit_bytes=8 << 20),
        cost_estimate=pl.CostEstimate(
            flops=2 * batch * features * half, bytes_accessed=features * half * 2, transcendentals=0
        ),
        name="own_product",
    )(ordered, strip, pltpu.with_memory_space_constraint(weight, pltpu.HBM))


def join_kernel(own, arrived, out):
    out[...] = (own[...] + arrived[...].astype(F32)).reshape(out.shape).astype(BF16)


def second_kernel(arrived, tile, out):
    half = arrived.shape[2]
    summed = arrived[...].astype(F32).sum(axis=0).astype(BF16)
    for i in range(out.shape[0]):
        out[i, :, :half] = summed
        out[i, :, half:] = tile[...]


def third_kernel(half, tail, arrived, out):
    yhs, yas, zas = (lax.axis_size(a) for a in FAR)
    piece = arrived.shape[1]
    total = arrived[:, :, :half].astype(F32).sum(axis=0).astype(BF16)
    upper = lax.broadcasted_iota(jnp.int32, (piece, LANES), 0) < piece // yas
    parts, tails = [total], jnp.zeros((piece, LANES), F32)
    for za in range(zas):
        for yh in range(yhs):
            low, high = (
                arrived[(yh * yas + ya) * zas + za, :, half:].astype(F32) for ya in range(yas)
            )
            parts.append(jnp.where(upper, low, pltpu.roll(high, piece // yas, 0)).astype(BF16))
            rest = jnp.where(upper, pltpu.roll(low, piece // yas, 0), high)
            shift = (za * yhs + yh) * tail
            tails += pltpu.roll(rest, shift, 1) if shift else rest
    parts.append(tails.astype(BF16))
    payload = jnp.concatenate(parts, axis=1)
    for i in range(out.shape[0]):
        out[i] = payload


def tail_rows(source, half, tail):
    xs, yhs, zas = (lax.axis_size(a) for a in ("x", "yh", "za"))
    depth = source.shape[0] // zas
    lane = lax.broadcasted_iota(jnp.int32, (depth, LANES), 1) // (yhs * tail)
    pieces = [
        source[x * depth : (x + 1) * depth, half + zas * yhs * LANES :].astype(F32)
        for x in range(xs)
    ]
    blocks = []
    for za in range(zas):
        block = jnp.zeros((depth, LANES), F32)
        for x in range(xs):
            shift = (x - za) * yhs * tail % LANES
            moved = pltpu.roll(pieces[x], shift, 1) if shift else pieces[x]
            block = jnp.where(lane == x, moved, block)
        blocks.append(block.astype(BF16))
    return jnp.concatenate(blocks, axis=0)


def near_kernel(tail, own, pre, weight, decoder_out, backward, tails, decoder, sems):
    features, half = decoder.shape
    core = lax.axis_index("core")
    hidden = jnp.maximum(pre[...], jnp.zeros_like(pre[...]))
    columns = pl.ds(pl.multiple_of(core * half, LANES), half)
    copies = []
    for i in range(2):
        part = slice(i * features // 2, (i + 1) * features // 2)
        decoder[part, :] = dot(hidden[:, part], own[:, :half], (0, 0)).astype(BF16)
        copies.append(
            pltpu.make_async_copy(decoder.at[part], decoder_out.at[part, columns], sems.at[i])
        )
        copies[-1].start()
    backward[...] = dot(own[:, :half], weight[:, columns], (1, 1))
    tails[...] = tail_rows(own, half, tail)
    for copy in copies:
        copy.wait()


def near_products(own, pre, weight, tail):
    features, width = weight.shape
    half = width // lax.axis_size("core")
    return pl.pallas_call(
        functools.partial(near_kernel, tail),
        out_shape=(
            pltpu.HBM((features, width), BF16),
            pltpu.VMEM(pre.shape, F32),
            pltpu.VMEM((pre.shape[0], LANES), BF16),
        ),
        in_specs=[VMEM] * 3,
        out_specs=(pl.BlockSpec(memory_space=pltpu.HBM), VMEM, VMEM),
        scratch_shapes=[pltpu.VMEM((features, half), BF16), pltpu.SemaphoreType.DMA((2,))],
        compiler_params=pltpu.CompilerParams(vmem_limit_bytes=10 << 20),
        cost_estimate=pl.CostEstimate(
            flops=4 * pre.shape[0] * features * half,
            bytes_accessed=features * width * 2,
            transcendentals=0,
        ),
        name="near_products",
    )(own, pre, weight)


def last_kernel(
    tail, own, other, pre, weight, backward, tails, _, decoder_out, encoder_out, decoder, encoder, sems
):
    batch, (features, half) = other.shape[0], decoder.shape
    core = lax.axis_index("core")
    cores, xs, yhs, zas = (lax.axis_size(a) for a in ("core", "x", "yh", "za"))
    depth, span = batch // zas, LANES + tail
    sources = ((own, core), (other, 1 - core))
    columns = pl.ds(pl.multiple_of((1 - core) * half, LANES), half)
    copies = []
    for i in range(2):
        part = slice(i * features // 2, (i + 1) * features // 2)
        copies.append(
            pltpu.make_async_copy(decoder.at[part], decoder_out.at[part, columns], sems.at[i])
        )

    @pl.when(core < cores)
    def _():
        hidden = jnp.maximum(pre[...], jnp.zeros_like(pre[...]))
        for i in range(2):
            part = slice(i * features // 2, (i + 1) * features // 2)
            decoder[part, :] = dot(hidden[:, part], other[:, :half], (0, 0)).astype(BF16)
            copies[i].start()

    total = backward[...] + dot(other[:, :half], weight[:, columns], (1, 1))
    masked = jnp.where(pre[...] > 0, total, jnp.zeros_like(total)).astype(BF16)
    rows = (tails[...], tail_rows(other, half, tail))
    ends = [dot(r, masked, (0, 0)).astype(BF16) for r in rows]
    for x in range(xs):
        for k, (source, c) in enumerate(sources):
            size = yhs * LANES
            part = [
                source[x * depth : (x + 1) * depth, half + za * size : half + (za + 1) * size]
                for za in range(zas)
            ]
            product = dot(jnp.concatenate(part, axis=0), masked, (0, 0)).astype(BF16)
            for yh in range(yhs):
                start = pl.multiple_of(((x * yhs + yh) * cores + c) * span, tail)
                encoder[pl.ds(start, LANES), :] = product[yh * LANES : (yh + 1) * LANES]
                end = (x * yhs + yh) * tail
                encoder[pl.ds(pl.multiple_of(start + LANES, tail), tail), :] = ends[k][end : end + tail]
        block = pl.ds(x * yhs * cores * span, yhs * cores * span)
        copies.append(
            pltpu.make_async_copy(encoder.at[block], encoder_out.at[block], sems.at[len(copies)])
        )
        copies[-1].start()
    for copy in copies:
        copy.wait()


def last_products(own, other, pre, weight, backward, tails, decoder, tail):
    features, width = weight.shape
    raw = pl.BlockSpec(memory_space=pltpu.HBM)
    return pl.pallas_call(
        functools.partial(last_kernel, tail),
        out_shape=(
            jax.ShapeDtypeStruct((features, width), BF16),
            jax.ShapeDtypeStruct((width, features), BF16),
        ),
        in_specs=[VMEM] * 6 + [raw],
        out_specs=(raw, raw),
        scratch_shapes=[
            pltpu.VMEM((features, width // lax.axis_size("core")), BF16),
            pltpu.VMEM((width, features), BF16),
            pltpu.SemaphoreType.DMA((2 + lax.axis_size("x"),)),
        ],
        input_output_aliases={6: 0},
        compiler_params=pltpu.CompilerParams(vmem_limit_bytes=20 << 20),
        name="last_products",
    )(own, other, pre, weight, backward, tails, decoder)


def shards(inputs, decoder_bias, preactivations, decoder_weight):
    columns = inputs.shape[1]
    batch, width = preactivations.shape[0], decoder_weight.shape[1]
    half = width // lax.axis_size("core")
    tail = columns - LANES
    near, far = lax.axis_size(NEAR), lax.axis_size(FAR)
    piece = batch // near
    partner = [(0, 1), (1, 0)]

    theirs, ordered, tile, strip = first_product(
        preactivations, decoder_weight, inputs, decoder_bias
    )
    arrived = lax.ppermute(theirs, "core", partner)
    mine = own_product(ordered, strip, decoder_weight)
    shape = jax.ShapeDtypeStruct((near, piece, half), BF16)
    arrived = swap(small_kernel(join_kernel, shape, 8, "join_cores", mine, arrived), NEAR)
    shape = jax.ShapeDtypeStruct((far, piece, half + LANES), BF16)
    arrived = swap(small_kernel(second_kernel, shape, 8, "second_sum", arrived, tile), FAR)
    shape = jax.ShapeDtypeStruct((near, piece, width), BF16)
    kernel = functools.partial(third_kernel, half, tail)
    own = swap(small_kernel(kernel, shape, 8, "third_sum", arrived), NEAR).reshape(batch, width)
    other = lax.ppermute(own, "core", partner)
    decoder, backward, tails = near_products(own, ordered, decoder_weight, tail)
    grad_decoder, grad_encoder = last_products(
        own, other, ordered, decoder_weight, backward, tails, decoder, tail
    )
    return (grad_encoder, grad_decoder)


def solution(mesh):
    split = Mesh(mesh.devices.reshape(SIZES), AXES)
    narrow, wide = AXES[:3], AXES[3:]
    return jax.shard_map(
        shards,
        mesh=split,
        in_specs=(P(wide, narrow), P(), P(None, narrow + wide), P(narrow + wide, None)),
        out_specs=(P(None, narrow + wide), P(narrow + wide, None)),
        check_vma=False,
    )
```

```python
import functools

import jax
import jax.numpy as jnp
from jax import lax
from jax.experimental import pallas as pl
from jax.experimental.pallas import tpu as pltpu
from jax.sharding import Mesh, PartitionSpec as P

BF16, F32 = jnp.bfloat16, jnp.float32
LANES, SUBLANES, CHUNKS = 128, 8, 3
AXES = ("x", "yh", "core", "ya", "yb", "za", "zb")
SIZES = (4, 2, 2, 2, 2, 4, 2)
NEAR, FAR = ("x", "yb", "zb"), ("yh", "ya", "za")
PLANE = ("yh", "ya", "yb", "za", "zb")
VMEM = pl.BlockSpec(memory_space=pltpu.VMEM)


def members(xs, ys, zs):
    return [(x * 8 + y) * 8 + z for x in xs for y in ys for z in zs]


def near_groups():
    pairs = [sorted((2 * k, 2 * k + 1), key=parity) for k in range(4)]
    return [members(range(4), ys, zs) for ys in pairs for zs in pairs]


def far_groups():
    sets = [[n for n in range(8) if parity(n) == side] for side in range(2)]
    return [members((0,), ys, zs) for ys in sets for zs in sets]


def swap(x, axis, groups):
    return lax.all_to_all(
        x, axis, split_axis=0, concat_axis=0, axis_index_groups=groups, tiled=True
    )


def dot(a, b, contract):
    return lax.dot_general(a, b, ((contract[:1], contract[1:]), ((), ())), preferred_element_type=F32)


def small_kernel(kernel, result, limit, name, *operands):
    return pl.pallas_call(
        kernel,
        out_shape=result,
        in_specs=[VMEM] * len(operands),
        out_specs=VMEM,
        compiler_params=pltpu.CompilerParams(vmem_limit_bytes=limit << 20),
        name=name,
    )(*operands)


def parity(n):
    return (n ^ (n >> 1) ^ (n >> 2)) & 1


def own_place(ya, yb, za, zb):
    return (za * 2 + (yb ^ ya)) * 2 + (zb ^ parity(za))


def row_order(batch, rows):
    shape = (batch, batch)
    new = lax.broadcasted_iota(jnp.int32, shape, 0)
    group, r = new // rows, lax.rem(new, rows)
    ya, group = lax.rem(group, 2), group // 2
    zb, group = lax.rem(group, 2), group // 2
    yb, za = lax.rem(group, 2), group // 2
    yb, zb = yb ^ ya, zb ^ parity(za)
    old = ((((ya * 2 + yb) * 4 + za) * 2) + zb) * rows + r
    return jnp.where(lax.broadcasted_iota(jnp.int32, shape, 1) == old, 1.0, 0.0).astype(BF16)


def first_kernel(
    pre_hbm, weight_hbm, inputs_hbm, bias_hbm, out, ordered, tile, strip, pre, weight, inputs, bias, sems
):
    batch, half = out.shape
    piece, width = strip.shape[0], bias.shape[0]
    rows, columns = inputs.shape
    step = half // CHUNKS
    x, yh, core, ya, yb, za, zb = (lax.axis_index(a) for a in AXES)
    there = (1 - core) * half
    pairs = [(inputs_hbm, inputs), (bias_hbm, bias), (pre_hbm, pre)]
    for i in range(CHUNKS):
        columns_there = pl.ds(pl.multiple_of(there + i * step, LANES), step)
        pairs.append((weight_hbm.at[:, columns_there], weight.at[:, pl.ds(i * step, step)]))
    copies = [pltpu.make_async_copy(a, b, sems.at[i]) for i, (a, b) in enumerate(pairs)]
    for copy in copies:
        copy.start()
    order = row_order(batch, rows)
    first = ((x * 2 + yh) * 2 + core) * columns
    copies[0].wait()
    copies[1].wait()
    whole = bias[...].reshape(1, width)
    here = pltpu.roll(whole, lax.rem(width - first, width), 1)[:, :columns]
    mine = inputs[...].astype(F32) - here
    spare = jnp.zeros((rows, 2 * LANES - columns), F32)
    padded = jnp.concatenate([mine, spare], axis=1)
    tile[...] = jnp.concatenate([padded[:, :LANES], padded[:, LANES:]], axis=0).astype(BF16)
    line = jnp.concatenate([mine, jnp.zeros((rows, half - columns), F32)], axis=1)
    line = jnp.concatenate([line, jnp.zeros((piece - rows, half), F32)], axis=0)
    strip[...] = pltpu.roll(pltpu.roll(line, lax.rem(first, half), 1), ya * rows, 0)
    copies[2].wait()
    ordered[...] = dot(order, pre[...], (1, 0)).astype(BF16)
    hidden = jnp.maximum(ordered[...], jnp.zeros_like(ordered[...]))
    place = jnp.where(first // half == core, batch, own_place(ya, yb, za, zb))
    for i in range(CHUNKS):
        copies[3 + i].wait()
        part = pl.ds(i * step, step)
        product = dot(hidden, weight[:, part], (1, 0))
        out[:, part] = less(product, strip[:, part], place).astype(BF16)


def less(product, strip, place):
    piece = strip.shape[0]
    pieces = product.reshape(product.shape[0] // piece, *strip.shape)
    owned = lax.broadcasted_iota(jnp.int32, pieces.shape, 0) == place
    pieces = pieces - jnp.where(owned, strip[None], jnp.zeros_like(strip)[None])
    return pieces.reshape(product.shape)


def first_product(pre, weight, inputs, bias):
    half = weight.shape[1] // lax.axis_size("core")
    operands = (pre, weight, inputs, bias)
    return pl.pallas_call(
        first_kernel,
        out_shape=(
            pltpu.VMEM((pre.shape[0], half), BF16),
            pltpu.VMEM(pre.shape, BF16),
            pltpu.VMEM((SUBLANES, LANES), BF16),
            pltpu.VMEM((SUBLANES, half), F32),
        ),
        in_specs=[pl.BlockSpec(memory_space=pltpu.HBM)] * 4,
        out_specs=(VMEM,) * 4,
        scratch_shapes=[
            pltpu.VMEM(pre.shape, BF16),
            pltpu.VMEM((weight.shape[0], half), BF16),
            pltpu.VMEM(inputs.shape, BF16),
            pltpu.VMEM(bias.shape, F32),
            pltpu.SemaphoreType.DMA((3 + CHUNKS,)),
        ],
        compiler_params=pltpu.CompilerParams(vmem_limit_bytes=12 << 20),
        name="first_product",
    )(*(pltpu.with_memory_space_constraint(a, pltpu.HBM) for a in operands))


def own_kernel(ordered, strip, weight_hbm, out, weight, sems):
    batch, half = out.shape
    step = half // CHUNKS
    x, yh, core, ya, yb, za, zb = (lax.axis_index(a) for a in AXES)
    copies = []
    for i in range(CHUNKS):
        columns = pl.ds(pl.multiple_of(core * half + i * step, LANES), step)
        target = weight.at[:, pl.ds(i * step, step)]
        copies.append(pltpu.make_async_copy(weight_hbm.at[:, columns], target, sems.at[i]))
        copies[-1].start()
    hidden = jnp.maximum(ordered[...], jnp.zeros_like(ordered[...]))
    place = jnp.where(x * 2 // lax.axis_size("x") == core, own_place(ya, yb, za, zb), batch)
    for i in range(CHUNKS):
        copies[i].wait()
        part = pl.ds(i * step, step)
        product = dot(hidden, weight[:, part], (1, 0))
        out[:, part] = less(product, strip[:, part], place)


def own_product(ordered, strip, weight):
    batch, features = ordered.shape
    half = strip.shape[1]
    return pl.pallas_call(
        own_kernel,
        out_shape=pltpu.VMEM((batch, half), F32),
        in_specs=[VMEM, VMEM, pl.BlockSpec(memory_space=pltpu.HBM)],
        out_specs=VMEM,
        scratch_shapes=[
            pltpu.VMEM((features, half), BF16),
            pltpu.SemaphoreType.DMA((CHUNKS,)),
        ],
        compiler_params=pltpu.CompilerParams(vmem_limit_bytes=8 << 20),
        cost_estimate=pl.CostEstimate(
            flops=2 * batch * features * half, bytes_accessed=features * half * 2, transcendentals=0
        ),
        name="own_product",
    )(ordered, strip, pltpu.with_memory_space_constraint(weight, pltpu.HBM))


def join_kernel(own, arrived, out):
    out[...] = (own[...] + arrived[...].astype(F32)).reshape(out.shape).astype(BF16)


def second_kernel(arrived, tile, out):
    half = arrived.shape[2]
    summed = arrived[...].astype(F32).sum(axis=0).astype(BF16)
    for i in range(out.shape[0]):
        out[i, :, :half] = summed
        out[i, :, half:] = tile[...]


def third_kernel(half, tail, arrived, out):
    yhs, yas, zas = (lax.axis_size(a) for a in FAR)
    piece = arrived.shape[1]
    total = arrived[:, :, :half].astype(F32).sum(axis=0).astype(BF16)
    upper = lax.broadcasted_iota(jnp.int32, (piece, LANES), 0) < piece // yas
    parts, tails = [total], jnp.zeros((piece, LANES), F32)
    for za in range(zas):
        for yh in range(yhs):
            low, high = (
                arrived[(yh * yas + ya) * zas + za, :, half:].astype(F32) for ya in range(yas)
            )
            parts.append(jnp.where(upper, low, pltpu.roll(high, piece // yas, 0)).astype(BF16))
            rest = jnp.where(upper, pltpu.roll(low, piece // yas, 0), high)
            shift = (za * yhs + yh) * tail
            tails += pltpu.roll(rest, shift, 1) if shift else rest
    parts.append(tails.astype(BF16))
    payload = jnp.concatenate(parts, axis=1)
    for i in range(out.shape[0]):
        out[i] = payload


def tail_rows(source, half, tail):
    xs, yhs, zas = (lax.axis_size(a) for a in ("x", "yh", "za"))
    depth = source.shape[0] // zas
    lane = lax.broadcasted_iota(jnp.int32, (depth, LANES), 1) // (yhs * tail)
    pieces = [
        source[x * depth : (x + 1) * depth, half + zas * yhs * LANES :].astype(F32)
        for x in range(xs)
    ]
    blocks = []
    for za in range(zas):
        block = jnp.zeros((depth, LANES), F32)
        for x in range(xs):
            shift = (x - za) * yhs * tail % LANES
            moved = pltpu.roll(pieces[x], shift, 1) if shift else pieces[x]
            block = jnp.where(lane == x, moved, block)
        blocks.append(block.astype(BF16))
    return jnp.concatenate(blocks, axis=0)


def block_rows(source, x, half):
    yhs, zas = lax.axis_size("yh"), lax.axis_size("za")
    depth, size = source.shape[0] // zas, yhs * LANES
    part = [
        source[x * depth : (x + 1) * depth, half + za * size : half + (za + 1) * size]
        for za in range(zas)
    ]
    return jnp.concatenate(part, axis=0)


def near_kernel(tail, own, pre, weight, decoder_out, backward, turned, flipped, decoder, sems):
    features, half = decoder.shape
    core = lax.axis_index("core")
    xs, size = lax.axis_size("x"), lax.axis_size("yh") * LANES
    flipped[...] = jnp.maximum(pre[...], jnp.zeros_like(pre[...])).T
    columns = pl.ds(pl.multiple_of(core * half, LANES), half)
    copies = []
    for i in range(2):
        part = slice(i * features // 2, (i + 1) * features // 2)
        decoder[part, :] = dot(flipped[part, :], own[:, :half], (1, 0)).astype(BF16)
        copies.append(
            pltpu.make_async_copy(decoder.at[part], decoder_out.at[part, columns], sems.at[i])
        )
        copies[-1].start()
    backward[...] = dot(own[:, :half], weight[:, columns], (1, 1))
    for x in range(xs):
        turned[x * size : (x + 1) * size, :] = block_rows(own, x, half).T
    turned[xs * size :, :] = tail_rows(own, half, tail).T
    for copy in copies:
        copy.wait()


def near_products(own, pre, weight, tail):
    features, width = weight.shape
    batch = pre.shape[0]
    half = width // lax.axis_size("core")
    return pl.pallas_call(
        functools.partial(near_kernel, tail),
        out_shape=(
            pltpu.HBM((features, width), BF16),
            pltpu.VMEM(pre.shape, F32),
            pltpu.VMEM((half, batch), BF16),
            pltpu.VMEM((features, batch), BF16),
        ),
        in_specs=[VMEM] * 3,
        out_specs=(pl.BlockSpec(memory_space=pltpu.HBM), VMEM, VMEM, VMEM),
        scratch_shapes=[pltpu.VMEM((features, half), BF16), pltpu.SemaphoreType.DMA((2,))],
        compiler_params=pltpu.CompilerParams(vmem_limit_bytes=10 << 20),
        cost_estimate=pl.CostEstimate(
            flops=4 * batch * features * half,
            bytes_accessed=features * width * 2,
            transcendentals=0,
        ),
        name="near_products",
    )(own, pre, weight)


def last_kernel(
    tail, other, pre, weight, backward, turned, flipped, _, decoder_out, encoder_out, decoder, encoder, sems
):
    half = decoder.shape[1]
    core = lax.axis_index("core")
    cores, xs, yhs = (lax.axis_size(a) for a in ("core", "x", "yh"))
    span, size = LANES + tail, yhs * LANES
    copies = []

    def send(source, target):
        copies.append(pltpu.make_async_copy(source, target, sems.at[len(copies)]))
        copies[-1].start()

    columns = pl.ds(pl.multiple_of((1 - core) * half, LANES), half)
    residual = other[:, :half]
    total = backward[...] + dot(residual, weight[:, columns], (1, 1))
    masked = jnp.where(pre[...] > 0, total, jnp.zeros_like(total)).astype(BF16)
    decoder[...] = dot(flipped[...], residual, (1, 0)).astype(BF16)
    send(decoder, decoder_out.at[:, columns])
    depth = masked.shape[0] // (2 * lax.axis_size("za"))
    swapped = [masked[(i ^ 1) * depth : ((i ^ 1) + 1) * depth] for i in range(masked.shape[0] // depth)]
    met = (masked, jnp.concatenate(swapped, axis=0))
    other_tails = tail_rows(other, half, tail)
    own_ends = [dot(turned[xs * size :, :], m, (1, 0)).astype(BF16) for m in met]
    other_ends = [dot(other_tails, m, (0, 0)).astype(BF16) for m in met]
    for x in range(xs):
        theirs = block_rows(other, x, half)
        for yh, m in enumerate(met):
            first = x * size + yh * LANES
            own_block = dot(turned[first : first + LANES, :], m, (1, 0)).astype(BF16)
            other_block = dot(theirs[:, yh * LANES : (yh + 1) * LANES], m, (0, 0)).astype(BF16)
            end = (x * yhs + yh) * tail
            for block, ends, c in (
                (own_block, own_ends[yh], core),
                (other_block, other_ends[yh], 1 - core),
            ):
                start = pl.multiple_of(((x * yhs + yh) * cores + c) * span, tail)
                encoder[pl.ds(start, LANES), :] = block
                encoder[pl.ds(pl.multiple_of(start + LANES, tail), tail), :] = ends[end : end + tail]
        rows = pl.ds(x * yhs * cores * span, yhs * cores * span)
        send(encoder.at[rows], encoder_out.at[rows])
    for copy in copies:
        copy.wait()


def last_products(other, pre, weight, near, tail):
    decoder, *rest = near
    features, width = weight.shape
    raw = pl.BlockSpec(memory_space=pltpu.HBM)
    return pl.pallas_call(
        functools.partial(last_kernel, tail),
        out_shape=(
            jax.ShapeDtypeStruct((features, width), BF16),
            jax.ShapeDtypeStruct((width, features), BF16),
        ),
        in_specs=[VMEM] * 6 + [raw],
        out_specs=(raw, raw),
        scratch_shapes=[
            pltpu.VMEM((features, width // lax.axis_size("core")), BF16),
            pltpu.VMEM((width, features), BF16),
            pltpu.SemaphoreType.DMA((1 + lax.axis_size("x"),)),
        ],
        input_output_aliases={6: 0},
        compiler_params=pltpu.CompilerParams(vmem_limit_bytes=20 << 20),
        name="last_products",
    )(other, pre, weight, *rest, decoder)


def shards(inputs, decoder_bias, preactivations, decoder_weight):
    columns = inputs.shape[1]
    batch, width = preactivations.shape[0], decoder_weight.shape[1]
    half = width // lax.axis_size("core")
    tail = columns - LANES
    near, far = lax.axis_size(NEAR), lax.axis_size(FAR)
    piece = batch // near
    partner = [(0, 1), (1, 0)]

    theirs, ordered, tile, strip = first_product(
        preactivations, decoder_weight, inputs, decoder_bias
    )
    arrived = lax.ppermute(theirs, "core", partner)
    mine = own_product(ordered, strip, decoder_weight)
    shape = jax.ShapeDtypeStruct((near, piece, half), BF16)
    arrived = swap(small_kernel(join_kernel, shape, 8, "join_cores", mine, arrived), ("x", *PLANE), near_groups())
    shape = jax.ShapeDtypeStruct((far, piece, half + LANES), BF16)
    arrived = swap(small_kernel(second_kernel, shape, 8, "second_sum", arrived, tile), PLANE, far_groups())
    shape = jax.ShapeDtypeStruct((near, piece, width), BF16)
    kernel = functools.partial(third_kernel, half, tail)
    own = small_kernel(kernel, shape, 8, "third_sum", arrived)
    own = swap(own, ("x", *PLANE), near_groups()).reshape(batch, width)
    other = lax.ppermute(own, "core", partner)
    near_part = near_products(own, ordered, decoder_weight, tail)
    grad_decoder, grad_encoder = last_products(other, ordered, decoder_weight, near_part, tail)
    return (grad_encoder, grad_decoder)


def solution(mesh):
    split = Mesh(mesh.devices.reshape(SIZES), AXES)
    narrow, wide = AXES[:3], AXES[3:]
    return jax.shard_map(
        shards,
        mesh=split,
        in_specs=(P(wide, narrow), P(), P(None, narrow + wide), P(narrow + wide, None)),
        out_specs=(P(None, narrow + wide), P(narrow + wide, None)),
        check_vma=False,
    )
```

```python
import functools

import jax
import jax.numpy as jnp
from jax import lax
from jax.experimental import pallas as pl
from jax.experimental.pallas import tpu as pltpu
from jax.sharding import Mesh, PartitionSpec as P

BF16, F32 = jnp.bfloat16, jnp.float32
LANES, SUBLANES, CHUNKS, PARTS = 128, 8, 3, 1
AXES = ("x", "yh", "core", "ya", "yb", "za", "zb")
SIZES = (4, 2, 2, 2, 2, 4, 2)
NEAR, FAR = ("x", "yb", "zb"), ("yh", "ya", "za")
PLANE = ("yh", "ya", "yb", "za", "zb")
VMEM = pl.BlockSpec(memory_space=pltpu.VMEM)


def members(xs, ys, zs):
    return [(x * 8 + y) * 8 + z for x in xs for y in ys for z in zs]


def near_groups():
    pairs = [sorted((2 * k, 2 * k + 1), key=parity) for k in range(4)]
    return [members(range(4), ys, zs) for ys in pairs for zs in pairs]


def far_groups():
    sets = [[n for n in range(8) if parity(n) == side] for side in range(2)]
    return [members((0,), ys, zs) for ys in sets for zs in sets]


def swap(x, axis, groups):
    return lax.all_to_all(
        x, axis, split_axis=0, concat_axis=0, axis_index_groups=groups, tiled=True
    )


def dot(a, b, contract):
    return lax.dot_general(a, b, ((contract[:1], contract[1:]), ((), ())), preferred_element_type=F32)


def small_kernel(kernel, result, limit, name, *operands):
    return pl.pallas_call(
        kernel,
        out_shape=result,
        in_specs=[VMEM] * len(operands),
        out_specs=VMEM,
        compiler_params=pltpu.CompilerParams(vmem_limit_bytes=limit << 20),
        name=name,
    )(*operands)


def parity(n):
    return (n ^ (n >> 1) ^ (n >> 2)) & 1


def own_place(ya, yb, za, zb):
    return (za * 2 + (yb ^ ya)) * 2 + (zb ^ parity(za))


def row_order(batch, rows):
    shape = (batch, batch)
    new = lax.broadcasted_iota(jnp.int32, shape, 0)
    group, r = new // rows, lax.rem(new, rows)
    ya, group = lax.rem(group, 2), group // 2
    zb, group = lax.rem(group, 2), group // 2
    yb, za = lax.rem(group, 2), group // 2
    yb, zb = yb ^ ya, zb ^ parity(za)
    old = ((((ya * 2 + yb) * 4 + za) * 2) + zb) * rows + r
    return jnp.where(lax.broadcasted_iota(jnp.int32, shape, 1) == old, 1.0, 0.0).astype(BF16)


def first_kernel(
    pre_hbm, weight_hbm, inputs_hbm, bias_hbm, out, ordered, tile, strip, pre, weight, inputs, bias, sems
):
    batch, half = out.shape
    piece, width = strip.shape[0], bias.shape[0]
    rows, columns = inputs.shape
    step = half // PARTS
    x, yh, core, ya, yb, za, zb = (lax.axis_index(a) for a in AXES)
    there = (1 - core) * half
    pairs = [(inputs_hbm, inputs), (bias_hbm, bias), (pre_hbm, pre)]
    for i in range(PARTS):
        columns_there = pl.ds(pl.multiple_of(there + i * step, LANES), step)
        pairs.append((weight_hbm.at[:, columns_there], weight.at[:, pl.ds(i * step, step)]))
    copies = [pltpu.make_async_copy(a, b, sems.at[i]) for i, (a, b) in enumerate(pairs)]
    for copy in copies:
        copy.start()
    order = row_order(batch, rows)
    first = ((x * 2 + yh) * 2 + core) * columns
    copies[0].wait()
    copies[1].wait()
    whole = bias[...].reshape(1, width)
    here = pltpu.roll(whole, lax.rem(width - first, width), 1)[:, :columns]
    mine = inputs[...].astype(F32) - here
    spare = jnp.zeros((rows, 2 * LANES - columns), F32)
    padded = jnp.concatenate([mine, spare], axis=1)
    tile[...] = jnp.concatenate([padded[:, :LANES], padded[:, LANES:]], axis=0).astype(BF16)
    line = jnp.concatenate([mine, jnp.zeros((rows, half - columns), F32)], axis=1)
    line = jnp.concatenate([line, jnp.zeros((piece - rows, half), F32)], axis=0)
    strip[...] = pltpu.roll(pltpu.roll(line, lax.rem(first, half), 1), ya * rows, 0)
    copies[2].wait()
    ordered[...] = dot(order, pre[...], (1, 0)).astype(BF16)
    hidden = jnp.maximum(ordered[...], jnp.zeros_like(ordered[...]))
    place = jnp.where(first // half == core, batch, own_place(ya, yb, za, zb))
    for i in range(PARTS):
        copies[3 + i].wait()
        part = pl.ds(i * step, step)
        product = dot(hidden, weight[:, part], (1, 0))
        out[:, part] = less(product, strip[:, part], place).astype(BF16)


def less(product, strip, place):
    piece = strip.shape[0]
    pieces = product.reshape(product.shape[0] // piece, *strip.shape)
    owned = lax.broadcasted_iota(jnp.int32, pieces.shape, 0) == place
    pieces = pieces - jnp.where(owned, strip[None], jnp.zeros_like(strip)[None])
    return pieces.reshape(product.shape)


def first_product(pre, weight, inputs, bias):
    half = weight.shape[1] // lax.axis_size("core")
    operands = (pre, weight, inputs, bias)
    return pl.pallas_call(
        first_kernel,
        out_shape=(
            pltpu.VMEM((pre.shape[0], half), BF16),
            pltpu.VMEM(pre.shape, BF16),
            pltpu.VMEM((SUBLANES, LANES), BF16),
            pltpu.VMEM((SUBLANES, half), F32),
        ),
        in_specs=[pl.BlockSpec(memory_space=pltpu.HBM)] * 4,
        out_specs=(VMEM,) * 4,
        scratch_shapes=[
            pltpu.VMEM(pre.shape, BF16),
            pltpu.VMEM((weight.shape[0], half), BF16),
            pltpu.VMEM(inputs.shape, BF16),
            pltpu.VMEM(bias.shape, F32),
            pltpu.SemaphoreType.DMA((3 + PARTS,)),
        ],
        compiler_params=pltpu.CompilerParams(vmem_limit_bytes=12 << 20),
        name="first_product",
    )(*(pltpu.with_memory_space_constraint(a, pltpu.HBM) for a in operands))


def own_kernel(ordered, strip, weight_hbm, out, weight, sems):
    batch, half = out.shape
    step = half // CHUNKS
    x, yh, core, ya, yb, za, zb = (lax.axis_index(a) for a in AXES)
    copies = []
    for i in range(CHUNKS):
        columns = pl.ds(pl.multiple_of(core * half + i * step, LANES), step)
        target = weight.at[:, pl.ds(i * step, step)]
        copies.append(pltpu.make_async_copy(weight_hbm.at[:, columns], target, sems.at[i]))
        copies[-1].start()
    hidden = jnp.maximum(ordered[...], jnp.zeros_like(ordered[...]))
    place = jnp.where(x * 2 // lax.axis_size("x") == core, own_place(ya, yb, za, zb), batch)
    for i in range(CHUNKS):
        copies[i].wait()
        part = pl.ds(i * step, step)
        product = dot(hidden, weight[:, part], (1, 0))
        out[:, part] = less(product, strip[:, part], place)


def own_product(ordered, strip, weight):
    batch, features = ordered.shape
    half = strip.shape[1]
    return pl.pallas_call(
        own_kernel,
        out_shape=pltpu.VMEM((batch, half), F32),
        in_specs=[VMEM, VMEM, pl.BlockSpec(memory_space=pltpu.HBM)],
        out_specs=VMEM,
        scratch_shapes=[
            pltpu.VMEM((features, half), BF16),
            pltpu.SemaphoreType.DMA((CHUNKS,)),
        ],
        compiler_params=pltpu.CompilerParams(vmem_limit_bytes=8 << 20),
        cost_estimate=pl.CostEstimate(
            flops=2 * batch * features * half, bytes_accessed=features * half * 2, transcendentals=0
        ),
        name="own_product",
    )(ordered, strip, pltpu.with_memory_space_constraint(weight, pltpu.HBM))


def join_kernel(own, arrived, out):
    out[...] = (own[...] + arrived[...].astype(F32)).reshape(out.shape).astype(BF16)


def second_kernel(arrived, tile, out):
    half = arrived.shape[2]
    summed = arrived[...].astype(F32).sum(axis=0).astype(BF16)
    for i in range(out.shape[0]):
        out[i, :, :half] = summed
        out[i, :, half:] = tile[...]


def third_kernel(half, tail, arrived, out):
    yhs, yas, zas = (lax.axis_size(a) for a in FAR)
    piece = arrived.shape[1]
    total = arrived[:, :, :half].astype(F32).sum(axis=0).astype(BF16)
    upper = lax.broadcasted_iota(jnp.int32, (piece, LANES), 0) < piece // yas
    parts, tails = [total], jnp.zeros((piece, LANES), F32)
    for za in range(zas):
        for yh in range(yhs):
            low, high = (
                arrived[(yh * yas + ya) * zas + za, :, half:].astype(F32) for ya in range(yas)
            )
            parts.append(jnp.where(upper, low, pltpu.roll(high, piece // yas, 0)).astype(BF16))
            rest = jnp.where(upper, pltpu.roll(low, piece // yas, 0), high)
            shift = (za * yhs + yh) * tail
            tails += pltpu.roll(rest, shift, 1) if shift else rest
    parts.append(tails.astype(BF16))
    payload = jnp.concatenate(parts, axis=1)
    for i in range(out.shape[0]):
        out[i] = payload


def tail_rows(source, half, tail):
    xs, yhs, zas = (lax.axis_size(a) for a in ("x", "yh", "za"))
    depth = source.shape[0] // zas
    lane = lax.broadcasted_iota(jnp.int32, (depth, LANES), 1) // (yhs * tail)
    pieces = [
        source[x * depth : (x + 1) * depth, half + zas * yhs * LANES :].astype(F32)
        for x in range(xs)
    ]
    blocks = []
    for za in range(zas):
        block = jnp.zeros((depth, LANES), F32)
        for x in range(xs):
            shift = (x - za) * yhs * tail % LANES
            moved = pltpu.roll(pieces[x], shift, 1) if shift else pieces[x]
            block = jnp.where(lane == x, moved, block)
        blocks.append(block.astype(BF16))
    return jnp.concatenate(blocks, axis=0)


def block_rows(source, x, half):
    yhs, zas = lax.axis_size("yh"), lax.axis_size("za")
    depth, size = source.shape[0] // zas, yhs * LANES
    part = [
        source[x * depth : (x + 1) * depth, half + za * size : half + (za + 1) * size]
        for za in range(zas)
    ]
    return jnp.concatenate(part, axis=0)


def near_kernel(
    tail, own, pre, weight, decoder_out, backward, turned, flipped, crossed, decoder, sems
):
    features, half = decoder.shape
    core = lax.axis_index("core")
    xs, size = lax.axis_size("x"), lax.axis_size("yh") * LANES
    flipped[...] = jnp.maximum(pre[...], jnp.zeros_like(pre[...])).T
    columns = pl.ds(pl.multiple_of(core * half, LANES), half)
    copies = []
    for i in range(2):
        part = slice(i * features // 2, (i + 1) * features // 2)
        decoder[part, :] = dot(flipped[part, :], own[:, :half], (1, 0)).astype(BF16)
        copies.append(
            pltpu.make_async_copy(decoder.at[part], decoder_out.at[part, columns], sems.at[i])
        )
        copies[-1].start()
    backward[...] = dot(own[:, :half], weight[:, columns], (1, 1))
    for x in range(xs):
        turned[x * size : (x + 1) * size, :] = block_rows(own, x, half).T
    turned[xs * size :, :] = tail_rows(own, half, tail).T
    crossed[...] = weight[:, pl.ds(pl.multiple_of((1 - core) * half, LANES), half)].T
    for copy in copies:
        copy.wait()


def near_products(own, pre, weight, tail):
    features, width = weight.shape
    batch = pre.shape[0]
    half = width // lax.axis_size("core")
    return pl.pallas_call(
        functools.partial(near_kernel, tail),
        out_shape=(
            pltpu.HBM((features, width), BF16),
            pltpu.VMEM(pre.shape, F32),
            pltpu.VMEM((half, batch), BF16),
            pltpu.VMEM((features, batch), BF16),
            pltpu.VMEM((half, features), BF16),
        ),
        in_specs=[VMEM] * 3,
        out_specs=(pl.BlockSpec(memory_space=pltpu.HBM),) + (VMEM,) * 4,
        scratch_shapes=[pltpu.VMEM((features, half), BF16), pltpu.SemaphoreType.DMA((2,))],
        compiler_params=pltpu.CompilerParams(vmem_limit_bytes=10 << 20),
        cost_estimate=pl.CostEstimate(
            flops=4 * batch * features * half,
            bytes_accessed=features * width * 2,
            transcendentals=0,
        ),
        name="near_products",
    )(own, pre, weight)


def last_kernel(
    tail, other, pre, backward, turned, flipped, crossed, _, decoder_out, encoder_out, decoder, encoder, sems
):
    half = decoder.shape[1]
    core = lax.axis_index("core")
    cores, xs, yhs = (lax.axis_size(a) for a in ("core", "x", "yh"))
    span, size = LANES + tail, yhs * LANES
    copies = []

    def send(source, target):
        copies.append(pltpu.make_async_copy(source, target, sems.at[len(copies)]))
        copies[-1].start()

    columns = pl.ds(pl.multiple_of((1 - core) * half, LANES), half)
    residual = other[:, :half]
    total = backward[...] + dot(residual, crossed[...], (1, 0))
    masked = jnp.where(pre[...] > 0, total, jnp.zeros_like(total)).astype(BF16)
    decoder[...] = dot(flipped[...], residual, (1, 0)).astype(BF16)
    send(decoder, decoder_out.at[:, columns])
    depth = masked.shape[0] // (2 * lax.axis_size("za"))
    swapped = [masked[(i ^ 1) * depth : ((i ^ 1) + 1) * depth] for i in range(masked.shape[0] // depth)]
    met = (masked, jnp.concatenate(swapped, axis=0))
    other_tails = tail_rows(other, half, tail)
    own_ends = [dot(turned[xs * size :, :], m, (1, 0)).astype(BF16) for m in met]
    other_ends = [dot(other_tails, m, (0, 0)).astype(BF16) for m in met]
    for x in range(xs):
        theirs = block_rows(other, x, half)
        for yh, m in enumerate(met):
            first = x * size + yh * LANES
            own_block = dot(turned[first : first + LANES, :], m, (1, 0)).astype(BF16)
            other_block = dot(theirs[:, yh * LANES : (yh + 1) * LANES], m, (0, 0)).astype(BF16)
            end = (x * yhs + yh) * tail
            for block, ends, c in (
                (own_block, own_ends[yh], core),
                (other_block, other_ends[yh], 1 - core),
            ):
                start = pl.multiple_of(((x * yhs + yh) * cores + c) * span, tail)
                encoder[pl.ds(start, LANES), :] = block
                encoder[pl.ds(pl.multiple_of(start + LANES, tail), tail), :] = ends[end : end + tail]
        rows = pl.ds(x * yhs * cores * span, yhs * cores * span)
        send(encoder.at[rows], encoder_out.at[rows])
    for copy in copies:
        copy.wait()


def last_products(other, pre, near, tail):
    decoder, *rest = near
    features, width = decoder.shape
    raw = pl.BlockSpec(memory_space=pltpu.HBM)
    return pl.pallas_call(
        functools.partial(last_kernel, tail),
        out_shape=(
            jax.ShapeDtypeStruct((features, width), BF16),
            jax.ShapeDtypeStruct((width, features), BF16),
        ),
        in_specs=[VMEM] * 6 + [raw],
        out_specs=(raw, raw),
        scratch_shapes=[
            pltpu.VMEM((features, width // lax.axis_size("core")), BF16),
            pltpu.VMEM((width, features), BF16),
            pltpu.SemaphoreType.DMA((1 + lax.axis_size("x"),)),
        ],
        input_output_aliases={6: 0},
        compiler_params=pltpu.CompilerParams(vmem_limit_bytes=20 << 20),
        name="last_products",
    )(other, pre, *rest, decoder)


def shards(inputs, decoder_bias, preactivations, decoder_weight):
    columns = inputs.shape[1]
    batch, width = preactivations.shape[0], decoder_weight.shape[1]
    half = width // lax.axis_size("core")
    tail = columns - LANES
    near, far = lax.axis_size(NEAR), lax.axis_size(FAR)
    piece = batch // near
    partner = [(0, 1), (1, 0)]

    theirs, ordered, tile, strip = first_product(
        preactivations, decoder_weight, inputs, decoder_bias
    )
    arrived = lax.ppermute(theirs, "core", partner)
    mine = own_product(ordered, strip, decoder_weight)
    shape = jax.ShapeDtypeStruct((near, piece, half), BF16)
    arrived = swap(small_kernel(join_kernel, shape, 8, "join_cores", mine, arrived), ("x", *PLANE), near_groups())
    shape = jax.ShapeDtypeStruct((far, piece, half + LANES), BF16)
    arrived = swap(small_kernel(second_kernel, shape, 8, "second_sum", arrived, tile), PLANE, far_groups())
    shape = jax.ShapeDtypeStruct((near, piece, width), BF16)
    kernel = functools.partial(third_kernel, half, tail)
    own = small_kernel(kernel, shape, 8, "third_sum", arrived)
    own = swap(own, ("x", *PLANE), near_groups()).reshape(batch, width)
    other = lax.ppermute(own, "core", partner)
    near_part = near_products(own, ordered, decoder_weight, tail)
    grad_decoder, grad_encoder = last_products(other, ordered, near_part, tail)
    return (grad_encoder, grad_decoder)


def solution(mesh):
    split = Mesh(mesh.devices.reshape(SIZES), AXES)
    narrow, wide = AXES[:3], AXES[3:]
    return jax.shard_map(
        shards,
        mesh=split,
        in_specs=(P(wide, narrow), P(), P(None, narrow + wide), P(narrow + wide, None)),
        out_specs=(P(None, narrow + wide), P(narrow + wide, None)),
        check_vma=False,
    )
```

```python
import functools

import jax
import jax.numpy as jnp
from jax import lax
from jax.experimental import pallas as pl
from jax.experimental.pallas import tpu as pltpu
from jax.sharding import Mesh, PartitionSpec as P

BF16, F32 = jnp.bfloat16, jnp.float32
LANES, SUBLANES, CHUNKS, PARTS = 128, 8, 1, 1
AXES = ("x", "yh", "core", "ya", "yb", "za", "zb")
SIZES = (4, 2, 2, 2, 2, 4, 2)
NEAR, FAR = ("x", "yb", "zb"), ("yh", "ya", "za")
PLANE = ("yh", "ya", "yb", "za", "zb")
VMEM = pl.BlockSpec(memory_space=pltpu.VMEM)


def members(xs, ys, zs):
    return [(x * 8 + y) * 8 + z for x in xs for y in ys for z in zs]


def near_groups():
    pairs = [sorted((2 * k, 2 * k + 1), key=parity) for k in range(4)]
    return [members(range(4), ys, zs) for ys in pairs for zs in pairs]


def far_groups():
    sets = [[n for n in range(8) if parity(n) == side] for side in range(2)]
    return [members((0,), ys, zs) for ys in sets for zs in sets]


def swap(x, axis, groups):
    return lax.all_to_all(
        x, axis, split_axis=0, concat_axis=0, axis_index_groups=groups, tiled=True
    )


def dot(a, b, contract):
    return lax.dot_general(a, b, ((contract[:1], contract[1:]), ((), ())), preferred_element_type=F32)


def small_kernel(kernel, result, limit, name, *operands):
    return pl.pallas_call(
        kernel,
        out_shape=result,
        in_specs=[VMEM] * len(operands),
        out_specs=VMEM,
        compiler_params=pltpu.CompilerParams(vmem_limit_bytes=limit << 20),
        name=name,
    )(*operands)


def parity(n):
    return (n ^ (n >> 1) ^ (n >> 2)) & 1


def own_place(ya, yb, za, zb):
    return (za * 2 + (yb ^ ya)) * 2 + (zb ^ parity(za))


def row_order(batch, rows):
    shape = (batch, batch)
    new = lax.broadcasted_iota(jnp.int32, shape, 0)
    group, r = new // rows, lax.rem(new, rows)
    ya, group = lax.rem(group, 2), group // 2
    zb, group = lax.rem(group, 2), group // 2
    yb, za = lax.rem(group, 2), group // 2
    yb, zb = yb ^ ya, zb ^ parity(za)
    old = ((((ya * 2 + yb) * 4 + za) * 2) + zb) * rows + r
    return jnp.where(lax.broadcasted_iota(jnp.int32, shape, 1) == old, 1.0, 0.0).astype(BF16)


def first_kernel(
    pre_hbm, weight_hbm, inputs_hbm, bias_hbm, out, ordered, tile, strip, pre, weight, inputs, bias, sems
):
    batch, half = out.shape
    piece, width = strip.shape[0], bias.shape[0]
    rows, columns = inputs.shape
    step = half // PARTS
    x, yh, core, ya, yb, za, zb = (lax.axis_index(a) for a in AXES)
    there = (1 - core) * half
    pairs = [(inputs_hbm, inputs), (bias_hbm, bias), (pre_hbm, pre)]
    for i in range(PARTS):
        columns_there = pl.ds(pl.multiple_of(there + i * step, LANES), step)
        pairs.append((weight_hbm.at[:, columns_there], weight.at[:, pl.ds(i * step, step)]))
    copies = [pltpu.make_async_copy(a, b, sems.at[i]) for i, (a, b) in enumerate(pairs)]
    for copy in copies:
        copy.start()
    order = row_order(batch, rows)
    first = ((x * 2 + yh) * 2 + core) * columns
    copies[0].wait()
    copies[1].wait()
    whole = bias[...].reshape(1, width)
    here = pltpu.roll(whole, lax.rem(width - first, width), 1)[:, :columns]
    mine = inputs[...].astype(F32) - here
    spare = jnp.zeros((rows, 2 * LANES - columns), F32)
    padded = jnp.concatenate([mine, spare], axis=1)
    tile[...] = jnp.concatenate([padded[:, :LANES], padded[:, LANES:]], axis=0).astype(BF16)
    line = jnp.concatenate([mine, jnp.zeros((rows, half - columns), F32)], axis=1)
    line = jnp.concatenate([line, jnp.zeros((piece - rows, half), F32)], axis=0)
    strip[...] = pltpu.roll(pltpu.roll(line, lax.rem(first, half), 1), ya * rows, 0)
    copies[2].wait()
    ordered[...] = dot(order, pre[...], (1, 0)).astype(BF16)
    hidden = jnp.maximum(ordered[...], jnp.zeros_like(ordered[...]))
    place = jnp.where(first // half == core, batch, own_place(ya, yb, za, zb))
    for i in range(PARTS):
        copies[3 + i].wait()
        part = pl.ds(i * step, step)
        product = dot(hidden, weight[:, part], (1, 0))
        out[:, part] = less(product, strip[:, part], place).astype(BF16)


def less(product, strip, place):
    piece = strip.shape[0]
    pieces = product.reshape(product.shape[0] // piece, *strip.shape)
    owned = lax.broadcasted_iota(jnp.int32, pieces.shape, 0) == place
    pieces = pieces - jnp.where(owned, strip[None], jnp.zeros_like(strip)[None])
    return pieces.reshape(product.shape)


def first_product(pre, weight, inputs, bias):
    half = weight.shape[1] // lax.axis_size("core")
    operands = (pre, weight, inputs, bias)
    return pl.pallas_call(
        first_kernel,
        out_shape=(
            pltpu.VMEM((pre.shape[0], half), BF16),
            pltpu.VMEM(pre.shape, BF16),
            pltpu.VMEM((SUBLANES, LANES), BF16),
            pltpu.VMEM((SUBLANES, half), F32),
        ),
        in_specs=[pl.BlockSpec(memory_space=pltpu.HBM)] * 4,
        out_specs=(VMEM,) * 4,
        scratch_shapes=[
            pltpu.VMEM(pre.shape, BF16),
            pltpu.VMEM((weight.shape[0], half), BF16),
            pltpu.VMEM(inputs.shape, BF16),
            pltpu.VMEM(bias.shape, F32),
            pltpu.SemaphoreType.DMA((3 + PARTS,)),
        ],
        compiler_params=pltpu.CompilerParams(vmem_limit_bytes=12 << 20),
        name="first_product",
    )(*(pltpu.with_memory_space_constraint(a, pltpu.HBM) for a in operands))


def own_kernel(ordered, strip, weight_hbm, out, weight, sems):
    batch, half = out.shape
    step = half // CHUNKS
    x, yh, core, ya, yb, za, zb = (lax.axis_index(a) for a in AXES)
    copies = []
    for i in range(CHUNKS):
        columns = pl.ds(pl.multiple_of(core * half + i * step, LANES), step)
        target = weight.at[:, pl.ds(i * step, step)]
        copies.append(pltpu.make_async_copy(weight_hbm.at[:, columns], target, sems.at[i]))
        copies[-1].start()
    hidden = jnp.maximum(ordered[...], jnp.zeros_like(ordered[...]))
    place = jnp.where(x * 2 // lax.axis_size("x") == core, own_place(ya, yb, za, zb), batch)
    for i in range(CHUNKS):
        copies[i].wait()
        part = pl.ds(i * step, step)
        product = dot(hidden, weight[:, part], (1, 0))
        out[:, part] = less(product, strip[:, part], place)


def own_product(ordered, strip, weight):
    batch, features = ordered.shape
    half = strip.shape[1]
    return pl.pallas_call(
        own_kernel,
        out_shape=pltpu.VMEM((batch, half), F32),
        in_specs=[VMEM, VMEM, pl.BlockSpec(memory_space=pltpu.HBM)],
        out_specs=VMEM,
        scratch_shapes=[
            pltpu.VMEM((features, half), BF16),
            pltpu.SemaphoreType.DMA((CHUNKS,)),
        ],
        compiler_params=pltpu.CompilerParams(vmem_limit_bytes=8 << 20),
        cost_estimate=pl.CostEstimate(
            flops=2 * batch * features * half, bytes_accessed=features * half * 2, transcendentals=0
        ),
        name="own_product",
    )(ordered, strip, pltpu.with_memory_space_constraint(weight, pltpu.HBM))


def join_kernel(own, arrived, out):
    out[...] = (own[...] + arrived[...].astype(F32)).reshape(out.shape).astype(BF16)


def second_kernel(arrived, tile, out):
    half = arrived.shape[2]
    summed = arrived[...].astype(F32).sum(axis=0).astype(BF16)
    for i in range(out.shape[0]):
        out[i, :, :half] = summed
        out[i, :, half:] = tile[...]


def third_kernel(half, tail, arrived, out):
    yhs, yas, zas = (lax.axis_size(a) for a in FAR)
    piece = arrived.shape[1]
    total = arrived[:, :, :half].astype(F32).sum(axis=0).astype(BF16)
    upper = lax.broadcasted_iota(jnp.int32, (piece, LANES), 0) < piece // yas
    parts, tails = [total], jnp.zeros((piece, LANES), F32)
    for za in range(zas):
        for yh in range(yhs):
            low, high = (
                arrived[(yh * yas + ya) * zas + za, :, half:].astype(F32) for ya in range(yas)
            )
            parts.append(jnp.where(upper, low, pltpu.roll(high, piece // yas, 0)).astype(BF16))
            rest = jnp.where(upper, pltpu.roll(low, piece // yas, 0), high)
            shift = (za * yhs + yh) * tail
            tails += pltpu.roll(rest, shift, 1) if shift else rest
    parts.append(tails.astype(BF16))
    payload = jnp.concatenate(parts, axis=1)
    for i in range(out.shape[0]):
        out[i] = payload


def tail_rows(source, half, tail):
    xs, yhs, zas = (lax.axis_size(a) for a in ("x", "yh", "za"))
    depth = source.shape[0] // zas
    lane = lax.broadcasted_iota(jnp.int32, (depth, LANES), 1) // (yhs * tail)
    pieces = [
        source[x * depth : (x + 1) * depth, half + zas * yhs * LANES :].astype(F32)
        for x in range(xs)
    ]
    blocks = []
    for za in range(zas):
        block = jnp.zeros((depth, LANES), F32)
        for x in range(xs):
            shift = (x - za) * yhs * tail % LANES
            moved = pltpu.roll(pieces[x], shift, 1) if shift else pieces[x]
            block = jnp.where(lane == x, moved, block)
        blocks.append(block.astype(BF16))
    return jnp.concatenate(blocks, axis=0)


def block_rows(source, x, half):
    yhs, zas = lax.axis_size("yh"), lax.axis_size("za")
    depth, size = source.shape[0] // zas, yhs * LANES
    part = [
        source[x * depth : (x + 1) * depth, half + za * size : half + (za + 1) * size]
        for za in range(zas)
    ]
    return jnp.concatenate(part, axis=0)


def near_kernel(
    tail, own, pre, weight, decoder_out, backward, turned, flipped, crossed, decoder, sems
):
    features, half = decoder.shape
    core = lax.axis_index("core")
    xs = lax.axis_size("x")
    flipped[...] = jnp.maximum(pre[...], jnp.zeros_like(pre[...])).T
    columns = pl.ds(pl.multiple_of(core * half, LANES), half)
    copies = []
    for i in range(2):
        part = slice(i * features // 2, (i + 1) * features // 2)
        decoder[part, :] = dot(flipped[part, :], own[:, :half], (1, 0)).astype(BF16)
        copies.append(
            pltpu.make_async_copy(decoder.at[part], decoder_out.at[part, columns], sems.at[i])
        )
        copies[-1].start()
    backward[...] = dot(own[:, :half], weight[:, columns], (1, 1))
    for x in range(xs):
        block = block_rows(own, x, half).T
        turned[x * LANES : (x + 1) * LANES, :] = block[:LANES]
        turned[half - (xs - x) * LANES : half - (xs - x - 1) * LANES, :] = block[LANES:]
    turned[xs * LANES : (xs + 1) * LANES, :] = tail_rows(own, half, tail).T
    crossed[...] = weight[:, pl.ds(pl.multiple_of((1 - core) * half, LANES), half)].T
    for copy in copies:
        copy.wait()


def near_products(own, pre, weight, tail):
    features, width = weight.shape
    batch = pre.shape[0]
    half = width // lax.axis_size("core")
    return pl.pallas_call(
        functools.partial(near_kernel, tail),
        out_shape=(
            pltpu.HBM((features, width), BF16),
            pltpu.VMEM(pre.shape, F32),
            pltpu.VMEM((half, batch), BF16),
            pltpu.VMEM((features, batch), BF16),
            pltpu.VMEM((half, features), BF16),
        ),
        in_specs=[VMEM] * 3,
        out_specs=(pl.BlockSpec(memory_space=pltpu.HBM),) + (VMEM,) * 4,
        scratch_shapes=[pltpu.VMEM((features, half), BF16), pltpu.SemaphoreType.DMA((2,))],
        compiler_params=pltpu.CompilerParams(vmem_limit_bytes=10 << 20),
        cost_estimate=pl.CostEstimate(
            flops=4 * batch * features * half,
            bytes_accessed=features * width * 2,
            transcendentals=0,
        ),
        name="near_products",
    )(own, pre, weight)


def last_kernel(
    tail, other, pre, backward, turned, flipped, crossed, _, decoder_out, encoder_out, decoder, encoder, sems
):
    half = decoder.shape[1]
    core = lax.axis_index("core")
    cores, xs, yhs = (lax.axis_size(a) for a in ("core", "x", "yh"))
    span = LANES + tail
    copies = []

    def send(source, target):
        copies.append(pltpu.make_async_copy(source, target, sems.at[len(copies)]))
        copies[-1].start()

    columns = pl.ds(pl.multiple_of((1 - core) * half, LANES), half)
    residual = other[:, :half]
    total = backward[...] + dot(residual, crossed[...], (1, 0))
    masked = jnp.where(pre[...] > 0, total, jnp.zeros_like(total)).astype(BF16)
    decoder[...] = dot(flipped[...], residual, (1, 0)).astype(BF16)
    send(decoder, decoder_out.at[:, columns])
    depth = masked.shape[0] // (2 * lax.axis_size("za"))
    swapped = [masked[(i ^ 1) * depth : ((i ^ 1) + 1) * depth] for i in range(masked.shape[0] // depth)]
    met = (masked, jnp.concatenate(swapped, axis=0))
    theirs = [block_rows(other, x, half) for x in range(xs)]
    other_tails = tail_rows(other, half, tail)
    for yh, m in enumerate(met):
        first = yh * xs * LANES
        lanes = [t[:, yh * LANES : (yh + 1) * LANES] for t in theirs]
        lanes = lanes + [other_tails] if yh == 0 else [other_tails] + lanes
        blocks = (
            (dot(turned[first : first + (xs + 1) * LANES, :], m, (1, 0)).astype(BF16), core),
            (dot(jnp.concatenate(lanes, axis=1), m, (0, 0)).astype(BF16), 1 - core),
        )
        for block, c in blocks:
            for x in range(xs):
                at = (x + yh) * LANES
                end = (0 if yh else xs * LANES) + (x * yhs + yh) * tail
                start = pl.multiple_of(((x * yhs + yh) * cores + c) * span, tail)
                encoder[pl.ds(start, LANES), :] = block[at : at + LANES]
                encoder[pl.ds(pl.multiple_of(start + LANES, tail), tail), :] = block[end : end + tail]
                send(encoder.at[pl.ds(start, span)], encoder_out.at[pl.ds(start, span)])
    for copy in copies:
        copy.wait()


def last_products(other, pre, near, tail):
    decoder, *rest = near
    features, width = decoder.shape
    raw = pl.BlockSpec(memory_space=pltpu.HBM)
    return pl.pallas_call(
        functools.partial(last_kernel, tail),
        out_shape=(
            jax.ShapeDtypeStruct((features, width), BF16),
            jax.ShapeDtypeStruct((width, features), BF16),
        ),
        in_specs=[VMEM] * 6 + [raw],
        out_specs=(raw, raw),
        scratch_shapes=[
            pltpu.VMEM((features, width // lax.axis_size("core")), BF16),
            pltpu.VMEM((width, features), BF16),
            pltpu.SemaphoreType.DMA((1 + width // (LANES + tail),)),
        ],
        input_output_aliases={6: 0},
        compiler_params=pltpu.CompilerParams(vmem_limit_bytes=20 << 20),
        name="last_products",
    )(other, pre, *rest, decoder)


def shards(inputs, decoder_bias, preactivations, decoder_weight):
    columns = inputs.shape[1]
    batch, width = preactivations.shape[0], decoder_weight.shape[1]
    half = width // lax.axis_size("core")
    tail = columns - LANES
    near, far = lax.axis_size(NEAR), lax.axis_size(FAR)
    piece = batch // near
    partner = [(0, 1), (1, 0)]

    theirs, ordered, tile, strip = first_product(
        preactivations, decoder_weight, inputs, decoder_bias
    )
    arrived = lax.ppermute(theirs, "core", partner)
    mine = own_product(ordered, strip, decoder_weight)
    shape = jax.ShapeDtypeStruct((near, piece, half), BF16)
    arrived = swap(small_kernel(join_kernel, shape, 8, "join_cores", mine, arrived), ("x", *PLANE), near_groups())
    shape = jax.ShapeDtypeStruct((far, piece, half + LANES), BF16)
    arrived = swap(small_kernel(second_kernel, shape, 8, "second_sum", arrived, tile), PLANE, far_groups())
    shape = jax.ShapeDtypeStruct((near, piece, width), BF16)
    kernel = functools.partial(third_kernel, half, tail)
    own = small_kernel(kernel, shape, 8, "third_sum", arrived)
    own = swap(own, ("x", *PLANE), near_groups()).reshape(batch, width)
    other = lax.ppermute(own, "core", partner)
    near_part = near_products(own, ordered, decoder_weight, tail)
    grad_decoder, grad_encoder = last_products(other, ordered, near_part, tail)
    return (grad_encoder, grad_decoder)


def solution(mesh):
    split = Mesh(mesh.devices.reshape(SIZES), AXES)
    narrow, wide = AXES[:3], AXES[3:]
    return jax.shard_map(
        shards,
        mesh=split,
        in_specs=(P(wide, narrow), P(), P(None, narrow + wide), P(narrow + wide, None)),
        out_specs=(P(None, narrow + wide), P(narrow + wide, None)),
        check_vma=False,
    )
```
